32 devices in a mesh: dp: 4 (over y, x), seq: 8 (over z, core).
Axes of the slice: x: 2, y: 2, z: 4, core: 2. Of those that a mesh axis runs over, the one named last changes fastest.
Arguments:
- query_rows: bfloat16 [4, 1024, 1536], P('dp', 'seq'), may hold values from -6 to 6
- key_rows: bfloat16 [4, 1024, 1536], P('dp', 'seq'), may hold values from -6 to 6
- value_rows: bfloat16 [4, 1024, 1536], P('dp', 'seq'), may hold values from -6 to 6
- out_grad: bfloat16 [4, 1024, 1536], P('dp', 'seq'), may hold values from -36 to 36
- query_gain: float32 [128], replicated, may hold values from 0.5 to 5.5
- key_gain: float32 [128], replicated, may hold values from 0.5 to 5.5
- lengths: int32 [4, 16], P('dp'), may hold values from 1 to 128, 1024 in all within a row
Outputs:
- query_grad: bfloat16 [4, 1024, 1536], P('dp', 'seq')
- key_grad: bfloat16 [4, 1024, 1536], P('dp', 'seq')
- value_grad: bfloat16 [4, 1024, 1536], P('dp', 'seq')
- gain_grads: float32 [2, 128], replicated
The draws below stay inside these ranges and needn't reach their ends.
Inputs may be any that keep to these rules, and one draw needn't show every extreme that they name: The 16 lengths of a pack sum to 1024, and some sample of every pack has exactly 128 tokens.
All inputs are finite; a program needn't handle non-finite values.
Results may differ from the reference program's by a relative error of at most 0.023.
The reference program's roundings to bfloat16 on the way count: a program that leaves them out, or rounds other values in their place, can miss the bound.
Values may be sent and summed in bfloat16 or wider, within the bound.
A program may use at most 64 MiB of HBM per device.

```python
import math
import jax
import jax.numpy as jnp
import numpy as np
from jax import lax

H = 12
DH = 128
SPAN = 1
TOK_DEV = 128
REACH = 128
PACKS = 4
PACK = 1024
NSAMP = 16
N_SEQ = 8


def key_field(key):
    field = jax.random.normal(jax.random.fold_in(key, 101), (PACKS, PACK, H * DH), jnp.float32)
    return jnp.clip(field, -6.0, 6.0)


def draw_key_rows(key, part):
    return key_field(key).astype(jnp.bfloat16)


def draw_query_rows(key, part):
    sampled = jax.random.normal(jax.random.fold_in(key, 107), (PACKS, PACK, H * DH), jnp.float32)
    return jnp.clip(sampled, -6.0, 6.0).astype(jnp.bfloat16)


def draw_out_grad(key, part):
    sampled = jnp.clip(jax.random.normal(jax.random.fold_in(key, 127), (PACKS, PACK, H * DH), jnp.float32), -4.0, 4.0)
    position = (jnp.arange(PACKS)[:, None] * PACK + jnp.arange(PACK)[None, :]).astype(jnp.float32) / (PACKS * PACK)
    factor = 3.0 ** position
    return (sampled * factor[:, :, None]).astype(jnp.bfloat16)


def gain_field(key, salt):
    spread = jax.random.uniform(jax.random.fold_in(key, salt), (DH,), jnp.float32)
    return 0.5 + spread


def draw_query_gain(key, part):
    return gain_field(key, 109)


def draw_key_gain(key, part):
    return gain_field(key, 113)


def level_of(stream_key, shape, pieces, low, largest):
    def one(axis_at, blocks):
        draws = jax.random.uniform(jax.random.fold_in(jax.random.fold_in(stream_key, 6), axis_at), (blocks,), jnp.float32, low / len(pieces), largest / len(pieces))
        return jnp.repeat(jnp.exp(draws), shape[axis_at] // blocks).reshape((-1,) + (1,) * (len(shape) - axis_at - 1))

    factor_of = one(*pieces[0])
    for cut in pieces[1:]:
        factor_of = factor_of * one(*cut)
    return factor_of


def length_profile(number_of, total, bound, skew):
    loads = [(1 << 20) // math.isqrt(rank ** skew) + 1 for rank in range(2, number_of + 1)]
    rest, holding = total - bound - (number_of - 1), [1] * (number_of - 1)
    while rest > 0:
        free = [i for i in range(number_of - 1) if holding[i] < bound]
        pool, left = sum([loads[i] for i in free]), rest
        for i in free:
            more = min(bound - holding[i], max(1, left * loads[i] // pool), rest)
            holding[i] = holding[i] + more
            rest = rest - more
    return np.array([bound] + holding)


def uneven_parts(key, count, total, bound, slope):
    if count == 2:
        one = jax.random.randint(key, (), max(1, total - bound), min(bound, total - 1) + 1)
        return jnp.stack([one, total - one])
    sizes = jnp.asarray(length_profile(count, total, bound, slope), jnp.int32)
    couples = (count - 1) // 2
    giver, receiver = sizes[1:1 + 2 * couples:2], sizes[2:2 + 2 * couples:2]
    room = jnp.minimum(giver - 1, bound - receiver)
    passed = jax.random.randint(jax.random.fold_in(key, 1), (couples,), 0, 1 << 20) % (room + 1)
    sizes = sizes.at[1:1 + 2 * couples:2].set(giver - passed).at[2:2 + 2 * couples:2].set(receiver + passed)
    return sizes[jax.random.permutation(jax.random.fold_in(key, 2), count)]


def scatter_about(stream_key, shape, scale, most, pieces=(), kind=jnp.bfloat16):
    values = jax.random.normal(stream_key, shape, jnp.float32) * scale
    if len(pieces) > 0:
        values = level_of(stream_key, shape, pieces, -0.22, 0.18) * values
    return jnp.clip(values, min=-most, max=most).astype(kind)


def setup_inputs(seed: int = 0) -> dict:
    arg_keys = jax.random.split(jax.random.key(seed), 8)
    query_rows = draw_query_rows(jax.random.fold_in(arg_keys[7], 71), 0)
    key_rows = draw_key_rows(jax.random.fold_in(arg_keys[7], 71), 0)
    value_rows = scatter_about(arg_keys[2], (PACKS, PACK, H * DH), 1.0, 6.0, ((0, 4), (1, 8)))
    out_grad = draw_out_grad(jax.random.fold_in(arg_keys[7], 71), 0)
    query_gain = draw_query_gain(jax.random.fold_in(arg_keys[7], 71), 0)
    key_gain = draw_key_gain(jax.random.fold_in(arg_keys[7], 71), 0)
    lengths = jax.vmap(lambda own: uneven_parts(own, NSAMP, PACK, REACH, 2))(jax.random.split(arg_keys[6], PACKS)).reshape((PACKS, NSAMP)).astype(jnp.int32)
    return dict(query_rows=query_rows, key_rows=key_rows, value_rows=value_rows, out_grad=out_grad, query_gain=query_gain, key_gain=key_gain, lengths=lengths)


EPSILON = 1e-06
MASKED = -1e+30

def product(pattern, left_side, right_side):
    return jnp.einsum(pattern, left_side.astype(jnp.float32), right_side.astype(jnp.float32))

def normalize(entries, norm_gain):
    row_count = entries.shape[0]
    widened = entries.astype(jnp.float32).reshape(row_count, H, DH)
    inverse = lax.rsqrt(lax.optimization_barrier(jnp.mean(widened * widened, axis=2, keepdims=True)) + EPSILON)
    unit_rows = widened * inverse
    return ((unit_rows * norm_gain).astype(jnp.bfloat16).reshape(row_count, H * DH), unit_rows, inverse)

def norm_back(grad_rows, unit_rows, inverse, norm_gain):
    scaled = grad_rows * norm_gain
    inner_mean = lax.optimization_barrier(jnp.mean(scaled * unit_rows, axis=2, keepdims=True))
    result = inverse * (scaled - unit_rows * inner_mean)
    return (result.reshape(grad_rows.shape[0], H * DH).astype(jnp.bfloat16), lax.optimization_barrier(jnp.sum(grad_rows * unit_rows, axis=(0, 1))))

def segment_of(positions, lengths, extent):
    sample_ends = jnp.cumsum(lengths)
    number = lax.optimization_barrier(jnp.sum((sample_ends[None, :] <= positions[:, None]).astype(jnp.int32), axis=1))
    inside = (positions >= 0) & (positions < extent)
    return jnp.where(inside, number, -1)

def forward_band(queries, band_keys, band_values, seg_query, seg_band):
    row_count = queries.shape[0]
    factor = DH ** (-0.5)
    scores = product('qhd,khd->hqk', queries.reshape(row_count, H, DH), band_keys.reshape(-1, H, DH)) * factor
    matching = seg_query[:, None] == seg_band[None, :]
    scores = jnp.where(matching[None], scores, MASKED)
    highest = lax.optimization_barrier(jnp.max(scores, axis=2, keepdims=True))
    summed = lax.optimization_barrier(jnp.sum(jnp.exp(scores - highest), axis=2, keepdims=True))
    log_total = highest + jnp.log(summed)
    weights = jnp.exp(scores - log_total)
    weights_half = weights.astype(jnp.bfloat16)
    attended = product('hqk,khd->qhd', weights_half, band_values.reshape(-1, H, DH)).astype(jnp.bfloat16)
    return (weights, weights_half, log_total, attended)

def backward_band(queries, band_keys, band_values, grad_out, weights, weights_half, attended):
    row_count = queries.shape[0]
    factor = DH ** (-0.5)
    grad_heads = grad_out.reshape(row_count, H, DH)
    row_dot = lax.optimization_barrier(jnp.sum(grad_heads.astype(jnp.float32) * attended.astype(jnp.float32), axis=2))
    row_dot = jnp.transpose(row_dot)[:, :, None]
    grad_weights = product('qhd,khd->hqk', grad_heads, band_values.reshape(-1, H, DH))
    grad_scores = (weights * (grad_weights - row_dot)).astype(jnp.bfloat16)
    grad_query = product('hqk,khd->qhd', grad_scores, band_keys.reshape(-1, H, DH)) * factor
    key_terms = product('hqk,qhd->khd', grad_scores, queries.reshape(row_count, H, DH)) * factor
    value_terms = product('hqk,qhd->khd', weights_half, grad_heads)
    return (grad_query, key_terms, value_terms)

def gather_rims(terms):
    blocks = terms.shape[0]
    split = terms.reshape(blocks, 2 * SPAN + 1, TOK_DEV, H, DH)
    summed = split[:, SPAN]
    for step in range(2 * SPAN + 1):
        if step != SPAN:
            move = step - SPAN
            piece = split[:, step]
            zeros = jnp.zeros_like(piece[:abs(move)])
            if move > 0:
                moved = jnp.concatenate([zeros, piece[:-move]], axis=0)
            else:
                moved = jnp.concatenate([piece[-move:], zeros], axis=0)
            summed = summed + moved
    return summed.reshape(PACK, H, DH)

def reference(query_rows, key_rows, value_rows, out_grad, query_gain, key_gain, lengths):

    def one_pack(operands):
        queries_in, keys_in, values_in, grads_in, pack_lengths = operands
        positions = jnp.arange(PACK, dtype=jnp.int32)
        segments = segment_of(positions, pack_lengths, PACK)
        q_norm, q_unit, q_inverse = normalize(queries_in, query_gain)
        k_norm, k_unit, k_inverse = normalize(keys_in, key_gain)
        zero_rows = jnp.zeros((REACH, H * DH), jnp.bfloat16)
        keys_padded = jnp.concatenate([zero_rows, k_norm, zero_rows], axis=0)
        values_padded = jnp.concatenate([zero_rows, values_in, zero_rows], axis=0)
        edge_segments = jnp.full((REACH,), -1, jnp.int32)
        seg_padded = jnp.concatenate([edge_segments, segments, edge_segments], axis=0)

        def one_block(block_index):
            block_start = (block_index * TOK_DEV).astype(jnp.int32)
            queries = lax.dynamic_slice_in_dim(q_norm, block_start, TOK_DEV, 0)
            grads = lax.dynamic_slice_in_dim(grads_in, block_start, TOK_DEV, 0)
            seg_query = lax.dynamic_slice_in_dim(segments, block_start, TOK_DEV, 0)
            band_keys = lax.dynamic_slice_in_dim(keys_padded, block_start, TOK_DEV + 2 * REACH, 0)
            band_values = lax.dynamic_slice_in_dim(values_padded, block_start, TOK_DEV + 2 * REACH, 0)
            seg_band = lax.dynamic_slice_in_dim(seg_padded, block_start, TOK_DEV + 2 * REACH, 0)
            weights, weights_half, log_total, attended = forward_band(queries, band_keys, band_values, seg_query, seg_band)
            return backward_band(queries, band_keys, band_values, grads, weights, weights_half, attended)
        grad_query, key_terms, value_terms = lax.map(one_block, jnp.arange(N_SEQ, dtype=jnp.int32))
        d_query, q_gain_grad = norm_back(grad_query.reshape(PACK, H, DH), q_unit, q_inverse, query_gain)
        d_key, k_gain_grad = norm_back(gather_rims(key_terms), k_unit, k_inverse, key_gain)
        d_value = gather_rims(value_terms).reshape(PACK, H * DH).astype(jnp.bfloat16)
        return (d_query, d_key, d_value, jnp.stack([q_gain_grad, k_gain_grad]))
    query_grad, key_grad, value_grad, gain_parts = lax.map(one_pack, (query_rows, key_rows, value_rows, out_grad, lengths))
    return (query_grad, key_grad, value_grad, lax.optimization_barrier(jnp.sum(gain_parts, axis=0)))
```

```python
import functools

import jax
import jax.numpy as jnp
from jax import lax
from jax.experimental import pallas as pl
from jax.experimental.pallas import tpu as pltpu
from jax.sharding import PartitionSpec as P

DH = 128
EPSILON = 1e-06
MASKED = -1e30
TILE = 16
GROUP = 4
SLOTS = GROUP - 1
LOG2E = 1.4426950408889634


def division(tiles):
    counts, most = [SLOTS], 0
    for left in range(1, tiles + 1):
        right = tiles + 1 - left
        need, taken = min((max(t * left, (GROUP - t) * right), -t) for t in range(1, GROUP))
        counts.append(-taken)
        most = max(most, need)
    return counts, most


def norm_back(grad, rows_in, inverse, gain):
    unit = rows_in * inverse
    scaled = grad * gain
    inner = jnp.mean(scaled * unit, axis=1, keepdims=True)
    return (inverse * (scaled - unit * inner)).astype(jnp.bfloat16)


def kernel(rows, width, samples, n_seq, n_dp, room, counts, *refs):
    heads = width // DH
    groups = heads // GROUP
    tiles = rows // TILE
    factor = DH ** (-0.5)
    refs = list(refs)

    def take(n):
        got = refs[:n]
        del refs[:n]
        return got

    q_in, k_in, v_in, g_in, qgain_in, kgain_in, len_in = take(7)
    dq_ref, dk_ref, dv_ref, gain_ref = take(4)
    qgain_ref, kgain_ref, len_ref = take(3)
    xq, xk, xv, xg, qn, kn, vt, gt, rinv, local, bias, owned, mine = take(13)
    fwd_send, ret_send, stage, gain_acc, seq_gain, dp_gain = take(6)
    fwd_recv = [take(groups) for _ in range(2)]
    ret_recv = [take(groups) for _ in range(2)]
    (load_sem, fwd_ss, fwd_rs, ret_ss, ret_rs, seq_ss, seq_rs, dp_ss, dp_rs) = take(9)

    me = lax.axis_index("seq")
    my_dp = lax.axis_index("dp")
    odd = lax.rem(me, 2)
    outputs = (dq_ref, dk_ref, dv_ref)

    barrier = pltpu.get_barrier_semaphore()
    for d in range(1, n_seq):
        pl.semaphore_signal(barrier, inc=1, device_id={"seq": lax.rem(me + d, n_seq)})
    for d in range(1, n_dp):
        pl.semaphore_signal(barrier, inc=1, device_id={"dp": lax.rem(my_dp + d, n_dp)})

    small = [
        pltpu.make_async_copy(src, dst, load_sem.at[4 + i])
        for i, (src, dst) in enumerate(((len_in, len_ref), (qgain_in, qgain_ref), (kgain_in, kgain_ref)))
    ]
    loads = [
        pltpu.make_async_copy(src.at[0], dst, load_sem.at[i])
        for i, (src, dst) in enumerate(((q_in, xq), (k_in, xk), (v_in, xv), (g_in, xg)))
    ]
    for load in small:
        load.start()
    for load in loads:
        load.start()
    for load in small:
        load.wait()

    right = (odd == 0, odd == 1)
    partner = (jnp.where(odd == 0, me - 1, me + 1), jnp.where(odd == 0, me + 1, me - 1))
    exists = tuple((p >= 0) & (p < n_seq) for p in partner)
    far = rows * n_seq + 2 * rows
    first = me * rows

    edge = [jnp.where(right[s], first, first + rows) for s in range(2)]
    start = [jnp.int32(0), jnp.int32(0)]
    end = [jnp.int32(far), jnp.int32(far)]
    col = lax.broadcasted_iota(jnp.int32, (rows, 1), 0)
    row = lax.broadcasted_iota(jnp.int32, (1, rows), 1)
    start_col = jnp.zeros((rows, 1), jnp.int32)
    start_row = jnp.zeros((1, rows), jnp.int32)
    total = jnp.int32(0)
    for i in range(samples):
        total = total + len_ref[0, i]
        for s in range(2):
            end[s] = jnp.where(total > edge[s], jnp.minimum(end[s], total), end[s])
            start[s] = jnp.where(total <= edge[s], total, start[s])
        start_col = jnp.where(total <= col + first, total, start_col)
        start_row = jnp.where(total <= row + first, total, start_row)

    def tile_count(n):
        return sum(jnp.where(n > t * TILE, 1, 0) for t in range(tiles))

    my_rows, far_rows, my_tiles, far_tiles, my_base, far_base, own_count = [], [], [], [], [], [], []
    for s in range(2):
        before = edge[s] - start[s]
        after = jnp.where(before > 0, end[s] - edge[s], 0)
        mr = jnp.where(right[s], after, before)
        fr = jnp.where(right[s], before, after)
        mt = tile_count(mr)
        ft = tile_count(fr)
        lt = jnp.where(right[s], ft, mt)
        taken = jnp.int32(counts[0])
        for n in range(1, len(counts)):
            if counts[n] != counts[n - 1]:
                taken = jnp.where(lt >= n, counts[n], taken)
        my_rows.append(mr)
        far_rows.append(fr)
        my_tiles.append(mt)
        far_tiles.append(ft)
        my_base.append(jnp.where(right[s], 0, tiles - mt))
        far_base.append(jnp.where(right[s], tiles - ft, 0))
        own_count.append(jnp.where(right[s], taken, GROUP - taken))

    def inside(s, at):
        low = jnp.where(right[s], 0, rows - my_rows[s])
        high = jnp.where(right[s], my_rows[s], rows)
        return (at >= low) & (at < high)

    def outside(s, at):
        low = jnp.where(right[s], rows - far_rows[s], 0)
        high = jnp.where(right[s], rows, far_rows[s])
        return (at >= low) & (at < high)

    bias[2] = jnp.where(start_col == start_row, 0.0, MASKED)
    owned[2] = jnp.where(inside(0, col) | inside(1, col), 0.0, 1.0)
    square = lax.broadcasted_iota(jnp.int32, (rows, DH), 0)
    for s in range(2):
        valid_col = inside(s, col) | outside(s, col)
        valid_row = inside(s, row) | outside(s, row)
        bias[s] = jnp.where(valid_col, 0.0, MASKED) + jnp.where(valid_row, 0.0, MASKED)
        owned[s] = jnp.where(valid_col, 1.0, 0.0)
        mine[s] = jnp.where(inside(s, square), 1.0, 0.0).astype(jnp.bfloat16)
    gain_acc[...] = jnp.zeros_like(gain_acc)

    for s in range(2):
        @pl.when(jnp.logical_not(exists[s]))
        def _(s=s):
            for g in range(groups):
                fwd_recv[s][g][...] = jnp.zeros_like(fwd_recv[s][g])
                ret_recv[s][g][...] = jnp.zeros_like(ret_recv[s][g])

    def columns(head):
        return pl.ds(pl.multiple_of(head * DH, DH), DH)

    def within(t):
        return jnp.where(t < 0, 0, jnp.where(t > room - 1, room - 1, t))

    def split(t, per):
        slot = jnp.int32(0)
        for n in range(1, SLOTS):
            slot = slot + jnp.where(t >= n * per, 1, 0)
        return slot, t - slot * per

    for load in loads[:2]:
        load.wait()

    @pl.loop(0, groups)
    def _(g):
        for i in range(GROUP):
            head = g * GROUP + i
            for n, (src, dst, gain) in enumerate(((xq, qn, qgain_ref), (xk, kn, kgain_ref))):
                x = src[:, columns(head)].astype(jnp.float32)
                r = lax.rsqrt(jnp.mean(x * x, axis=1, keepdims=True) + EPSILON)
                normed = (x * r * gain[...]).astype(jnp.bfloat16)
                dst[pl.ds(head * tiles, tiles)] = normed.reshape(tiles, TILE, DH)
                rinv[n, head] = jnp.broadcast_to(r, (rows, DH))

    for load in loads[2:]:
        load.wait()

    @pl.loop(0, groups)
    def _(g):
        for i in range(GROUP):
            head = g * GROUP + i
            for src, dst in ((xv, vt), (xg, gt)):
                dst[pl.ds(head * tiles, tiles)] = src[:, columns(head)].reshape(tiles, TILE, DH)

    operands = (qn, kn, vt, gt)

    def whole(ref, head):
        return ref[pl.ds(head * tiles, tiles)].reshape(rows, DH)

    out_slots = [[split(t, my_tiles[s]) for t in range(room)] for s in range(2)]
    back_slots = [[split(t, far_tiles[s]) for t in range(room)] for s in range(2)]

    def pack(s, g):
        for t in range(room):
            slot, at = out_slots[s][t]
            tile = my_base[s] + at
            tile = jnp.where(tile > tiles - 1, tiles - 1, tile)
            head = g * GROUP + jnp.where(right[s], GROUP - 1 - slot, slot)
            for a, ref in enumerate(operands):
                fwd_send[s, g, a, t] = ref[head * tiles + tile]

    def forward(s, g):
        return pltpu.make_async_remote_copy(
            fwd_send.at[s, g], fwd_recv[s][g], fwd_ss.at[s, g], fwd_rs.at[s, g], device_id={"seq": partner[s]}
        )

    def backward(s, g):
        return pltpu.make_async_remote_copy(
            ret_send.at[s, g], ret_recv[s][g], ret_ss.at[s, g], ret_rs.at[s, g], device_id={"seq": partner[s]}
        )

    for g in range(groups):
        pack(0, g)
    pl.semaphore_wait(barrier, n_seq + n_dp - 2)

    @pl.when(exists[0])
    def _():
        for g in range(groups):
            forward(0, g).start()

    for g in range(groups):
        pack(1, g)

    @pl.when(exists[1])
    def _():
        for g in range(groups):
            forward(1, g).start()

    rowrow = (((1,), (1,)), ((), ()))
    rowcol = (((1,), (0,)), ((), ()))
    colcol = (((0,), (0,)), ((), ()))
    dot = functools.partial(lax.dot_general, preferred_element_type=jnp.float32)

    def attend(blocks):
        scores = [dot(q, k, rowrow) * (factor * LOG2E) + bias_now for q, k, _, _, bias_now, _ in blocks]
        grad_weights = [dot(grad, v, rowrow) for _, _, v, grad, _, _ in blocks]
        highest = [jnp.max(x, axis=1, keepdims=True) for x in scores]
        powers = [jnp.exp2(x - y) for x, y in zip(scores, highest)]
        summed = [jnp.sum(x, axis=1, keepdims=True) for x in powers]
        weights = [x * (block[5] / y) for x, y, block in zip(powers, summed, blocks)]
        half_weights = [x.astype(jnp.bfloat16) for x in weights]
        attended = [dot(x, block[2], rowcol) for x, block in zip(half_weights, blocks)]
        dv = [dot(x, block[3], colcol) for x, block in zip(half_weights, blocks)]
        row_dot = [
            jnp.sum(block[3].astype(jnp.float32) * x.astype(jnp.bfloat16).astype(jnp.float32), axis=1, keepdims=True)
            for x, block in zip(attended, blocks)
        ]
        grad_scores = [(x * (y - z)).astype(jnp.bfloat16) for x, y, z in zip(weights, grad_weights, row_dot)]
        dq = [dot(x, block[1], rowcol) for x, block in zip(grad_scores, blocks)]
        dk = [dot(x, block[0], colcol) for x, block in zip(grad_scores, blocks)]
        for n, totals in enumerate((dq, dk)):
            terms = sum(x * block[n].astype(jnp.float32) for x, block in zip(totals, blocks))
            gain_acc[n] += jnp.sum(terms.reshape(rows // 8, 8, DH), axis=0)
        return [tuple(x.astype(jnp.bfloat16) for x in result) for result in zip(dq, dk, dv)]

    @pl.loop(0, groups)
    def _(g):
        spots = [g * GROUP + i for i in range(GROUP)]
        results = attend([(*(whole(ref, head) for ref in operands), bias[2], owned[2]) for head in spots])
        for head, result in zip(spots, results):
            for a in range(3):
                local[a, :, columns(head)] = result[a]

    def crossing(s, g):
        own = mine[s] > 0.5
        found = []
        for i in range(SLOTS):
            head = g * GROUP + jnp.where(right[s], i, GROUP - 1 - i)
            there = [
                within(i * far_tiles[s] + t - far_base[s]) for t in range(tiles)
            ]
            parts = []
            for a, ref in enumerate(operands):
                other = jnp.concatenate([fwd_recv[s][g][a, t] for t in there], axis=0)
                parts.append(jnp.where(own, whole(ref, head), other))
            real = jnp.where(i < own_count[s], 1.0, 0.0)
            found.append((*parts, bias[s], owned[s] * real))
        return found

    def pack_back(s, g):
        for t in range(room):
            slot, at = back_slots[s][t]
            tile = far_base[s] + at
            tile = jnp.where(tile > tiles - 1, tiles - 1, tile)
            for a in range(3):
                ret_send[s, g, a, t] = stage[s, g, a, slot * tiles + tile]

    for g in range(groups):
        for s in range(2):
            @pl.when(exists[s])
            def _(s=s, g=g):
                forward(s, g).wait_recv()
        results = attend(crossing(0, g) + crossing(1, g))
        for s in range(2):
            for i in range(SLOTS):
                for a in range(3):
                    stage[s, g, a, i * tiles:(i + 1) * tiles] = results[s * SLOTS + i][a].reshape(tiles, TILE, DH)
            pack_back(s, g)

            @pl.when(exists[s])
            def _(s=s, g=g):
                backward(s, g).start()

    def exchange(slots, axis, place, count, send_sems, recv_sems):
        def copy(d, slot):
            return pltpu.make_async_remote_copy(
                slots.at[place], slots.at[slot], send_sems.at[d], recv_sems.at[slot],
                device_id={axis: lax.rem(place + d, count)},
            )

        def start():
            for d in range(1, count):
                copy(d, place).start()

        def wait():
            for d in range(1, count):
                copy(d, lax.rem(place + d, count)).wait()
            total = slots[0]
            for i in range(1, count):
                total = total + slots[i]
            return total

        return start, wait

    dp_start, dp_wait = exchange(dp_gain, "dp", my_dp, n_dp, dp_ss, dp_rs)
    seq_start, seq_wait = exchange(seq_gain, "seq", me, n_seq, seq_ss, seq_rs)

    def merge(g):
        for s in range(2):
            @pl.when(exists[s])
            def _(s=s):
                backward(s, g).wait_recv()
        own_rows = [mine[s] > 0.5 for s in range(2)]
        for i in range(GROUP):
            head = g * GROUP + i
            cols = columns(head)
            merged = []
            for a in range(3):
                value = local[a, :, cols]
                for s in range(2):
                    slot = jnp.where(right[s], i, GROUP - 1 - i)
                    kept = stage[s, g, a, pl.ds(jnp.minimum(slot, SLOTS - 1) * tiles, tiles)].reshape(rows, DH)
                    there = [
                        within((GROUP - 1 - slot) * my_tiles[s] + t - my_base[s])
                        for t in range(tiles)
                    ]
                    back = jnp.concatenate([ret_recv[s][g][a, t] for t in there], axis=0)
                    ours = jnp.full((rows, DH), slot) < own_count[s]
                    chosen = jnp.where(ours, kept, back)
                    value = jnp.where(own_rows[s], chosen, value)
                merged.append(value)
            for n, (src, gain) in enumerate(((xq, qgain_ref), (xk, kgain_ref))):
                outputs[n][0, :, cols] = norm_back(
                    merged[n].astype(jnp.float32), src[:, cols].astype(jnp.float32), rinv[n, head], gain[...] * factor
                )
            dv_ref[0, :, cols] = merged[2]

    gains = (qgain_ref, kgain_ref)
    for n in range(2):
        dp_gain[my_dp, n:n + 1] = jnp.sum(gain_acc[n], axis=0, keepdims=True) * factor / gains[n][...]
    dp_start()
    merge(0)
    seq_gain[me] = dp_wait()
    seq_start()
    for g in range(1, groups):
        merge(g)
    gain_ref[...] = seq_wait()

    for s in range(2):
        @pl.when(exists[s])
        def _(s=s):
            for g in range(groups):
                forward(s, g).wait_send()
                backward(s, g).wait_send()


def write_back(dq_in, dk_in, dv_in, gain_in, dq_ref, dk_ref, dv_ref, gain_ref, sem):
    copies = [
        pltpu.make_async_copy(held, out, sem.at[i])
        for i, (held, out) in enumerate(
            ((dq_in, dq_ref), (dk_in, dk_ref), (dv_in, dv_ref), (gain_in, gain_ref))
        )
    ]
    for copy in copies:
        copy.start()
    for copy in copies:
        copy.wait()


def body(query_rows, key_rows, value_rows, out_grad, query_gain, key_gain, lengths):
    rows, width = query_rows.shape[1:]
    samples = lengths.shape[1]
    n_seq, n_dp = lax.axis_size("seq"), lax.axis_size("dp")
    heads = width // DH
    groups = heads // GROUP
    counts, room = division(rows // TILE)
    big = jax.ShapeDtypeStruct((1, rows, width), jnp.bfloat16)
    anywhere = pl.BlockSpec(memory_space=pl.ANY)
    hbm = pl.BlockSpec(memory_space=pltpu.HBM)
    vmem = pl.BlockSpec(memory_space=pltpu.VMEM)
    dma = pltpu.SemaphoreType.DMA
    half = jnp.bfloat16
    limit = 67043328 - 3 * big.size * 2 - 131072
    shapes = (big, big, big, jax.ShapeDtypeStruct((2, DH), jnp.float32))
    results = pl.pallas_call(
        functools.partial(kernel, rows, width, samples, n_seq, n_dp, room, counts),
        out_shape=tuple(pltpu.VMEM(x.shape, x.dtype) for x in shapes),
        in_specs=[hbm] * 4 + [hbm] * 3,
        out_specs=(vmem, vmem, vmem, vmem),
        scratch_shapes=[
            pltpu.VMEM((1, DH), jnp.float32),
            pltpu.VMEM((1, DH), jnp.float32),
            pltpu.SMEM((1, samples), jnp.int32),
            *[pltpu.VMEM((rows, width), half)] * 4,
            *[pltpu.VMEM((heads * rows // TILE, TILE, DH), half)] * 4,
            pltpu.VMEM((2, heads, rows, DH), jnp.float32),
            pltpu.VMEM((3, rows, width), half),
            pltpu.VMEM((3, rows, rows), jnp.float32),
            pltpu.VMEM((3, rows, 1), jnp.float32),
            pltpu.VMEM((2, rows, DH), half),
            pltpu.VMEM((2, groups, 4, room, TILE, DH), half),
            pltpu.VMEM((2, groups, 3, room, TILE, DH), half),
            pltpu.VMEM((2, groups, 3, SLOTS * rows // TILE, TILE, DH), half),
            pltpu.VMEM((2, 8, DH), jnp.float32),
            pltpu.VMEM((n_seq, 2, DH), jnp.float32),
            pltpu.VMEM((n_dp, 2, DH), jnp.float32),
            *[pltpu.VMEM((4, room, TILE, DH), half)] * (2 * groups),
            *[pltpu.VMEM((3, room, TILE, DH), half)] * (2 * groups),
            dma((7,)),
            dma((2, groups)),
            dma((2, groups)),
            dma((2, groups)),
            dma((2, groups)),
            dma((n_seq,)),
            dma((n_seq,)),
            dma((n_dp,)),
            dma((n_dp,)),
        ],
        compiler_params=pltpu.CompilerParams(collective_id=0, has_side_effects=True, vmem_limit_bytes=limit),
    )(
        query_rows, key_rows, value_rows, out_grad,
        query_gain.reshape(1, DH), key_gain.reshape(1, DH), lengths,
    )
    return pl.pallas_call(
        write_back,
        out_shape=shapes,
        in_specs=[anywhere] * 4,
        out_specs=(anywhere,) * 4,
        scratch_shapes=[dma((4,))],
        compiler_params=pltpu.CompilerParams(vmem_limit_bytes=8 << 20),
    )(*results)


def solution(mesh):
    placed = (
        P("dp", "seq", None),
        P("dp", "seq", None),
        P("dp", "seq", None),
        P("dp", "seq", None),
        P(),
        P(),
        P("dp", None),
    )
    return jax.shard_map(
        body,
        mesh=mesh,
        in_specs=placed,
        out_specs=(P("dp", "seq", None), P("dp", "seq", None), P("dp", "seq", None), P()),
        check_vma=False,
    )
```

```python
import functools

import jax
import jax.numpy as jnp
from jax import lax
from jax.experimental import pallas as pl
from jax.experimental.pallas import tpu as pltpu
from jax.sharding import PartitionSpec as P

DH = 128
EPSILON = 1e-06
MASKED = -1e30
TILE = 16
GROUP = 4
SLOTS = GROUP - 1
LOG2E = 1.4426950408889634


def division(tiles):
    counts, most = [SLOTS], 0
    for left in range(1, tiles + 1):
        right = tiles + 1 - left
        need, taken = min((max(t * left, (GROUP - t) * right), -t) for t in range(1, GROUP))
        counts.append(-taken)
        most = max(most, need)
    return counts, most


def norm_back(grad, rows_in, inverse, gain):
    unit = rows_in * inverse
    scaled = grad * gain
    inner = jnp.mean(scaled * unit, axis=1, keepdims=True)
    return (inverse * (scaled - unit * inner)).astype(jnp.bfloat16)


def kernel(rows, width, samples, n_seq, n_dp, room, counts, *refs):
    heads = width // DH
    groups = heads // GROUP
    tiles = rows // TILE
    factor = DH ** (-0.5)
    refs = list(refs)

    def take(n):
        got = refs[:n]
        del refs[:n]
        return got

    q_in, k_in, v_in, g_in, qgain_in, kgain_in, len_in = take(7)
    dq_ref, dk_ref, dv_ref, gain_ref = take(4)
    qgain_ref, kgain_ref, len_ref = take(3)
    xq, xk, xv, xg, qn, kn, vt, gt, rinv, local, bias, owned, mine = take(13)
    fwd_send, ret_send, stage, gain_acc, all_gain = take(5)
    fwd_recv = [take(groups) for _ in range(2)]
    ret_recv = [take(groups) for _ in range(2)]
    (load_sem, fwd_ss, fwd_rs, ret_ss, ret_rs, gain_ss, gain_rs, ready) = take(8)

    me = lax.axis_index("seq")
    my_dp = lax.axis_index("dp")
    odd = lax.rem(me, 2)
    outputs = (dq_ref, dk_ref, dv_ref)

    right = (odd == 0, odd == 1)
    partner = (jnp.where(odd == 0, me - 1, me + 1), jnp.where(odd == 0, me + 1, me - 1))
    exists = tuple((p >= 0) & (p < n_seq) for p in partner)

    def columns(head):
        return pl.ds(pl.multiple_of(head * DH, DH), DH)

    def span(g):
        return pl.ds(g * GROUP * DH, GROUP * DH)

    small = [
        pltpu.make_async_copy(src, dst, load_sem.at[groups, i])
        for i, (src, dst) in enumerate(((len_in, len_ref), (qgain_in, qgain_ref), (kgain_in, kgain_ref)))
    ]
    loads = [
        [
            pltpu.make_async_copy(src.at[0, :, span(g)], dst.at[:, span(g)], load_sem.at[g, i])
            for i, (src, dst) in enumerate(((q_in, xq), (k_in, xk), (v_in, xv), (g_in, xg)))
        ]
        for g in range(groups)
    ]

    barrier = pltpu.get_barrier_semaphore()
    for s in range(2):
        @pl.when(exists[s])
        def _(s=s):
            pl.semaphore_signal(barrier, inc=1, device_id={"seq": partner[s]})
    small[0].start()
    for load in loads[0]:
        load.start()
    for load in small[1:]:
        load.start()
    for g in range(1, groups):
        for load in loads[g]:
            load.start()
    for d in range(1, n_dp):
        pl.semaphore_signal(barrier, inc=1, device_id={"dp": lax.rem(my_dp + d, n_dp)})
    for d in range(1, n_seq):
        other = lax.rem(me + d, n_seq)

        @pl.when((other != partner[0]) & (other != partner[1]))
        def _(other=other):
            pl.semaphore_signal(barrier, inc=1, device_id={"seq": other})
    small[0].wait()

    far = rows * n_seq + 2 * rows
    first = me * rows

    edge = [jnp.where(right[s], first, first + rows) for s in range(2)]
    start = [jnp.int32(0), jnp.int32(0)]
    end = [jnp.int32(far), jnp.int32(far)]
    total = jnp.int32(0)
    for i in range(samples):
        total = total + len_ref[0, i]
        for s in range(2):
            end[s] = jnp.where(total > edge[s], jnp.minimum(end[s], total), end[s])
            start[s] = jnp.where(total <= edge[s], total, start[s])

    def tile_count(n):
        return sum(jnp.where(n > t * TILE, 1, 0) for t in range(tiles))

    my_rows, far_rows, my_tiles, far_tiles, my_base, far_base, own_count = [], [], [], [], [], [], []
    for s in range(2):
        before = edge[s] - start[s]
        after = jnp.where(before > 0, end[s] - edge[s], 0)
        mr = jnp.where(right[s], after, before)
        fr = jnp.where(right[s], before, after)
        mt = tile_count(mr)
        ft = tile_count(fr)
        lt = jnp.where(right[s], ft, mt)
        taken = jnp.int32(counts[0])
        for n in range(1, len(counts)):
            if counts[n] != counts[n - 1]:
                taken = jnp.where(lt >= n, counts[n], taken)
        my_rows.append(mr)
        far_rows.append(fr)
        my_tiles.append(mt)
        far_tiles.append(ft)
        my_base.append(jnp.where(right[s], 0, tiles - mt))
        far_base.append(jnp.where(right[s], tiles - ft, 0))
        own_count.append(jnp.where(right[s], taken, GROUP - taken))

    def inside(s, at):
        low = jnp.where(right[s], 0, rows - my_rows[s])
        high = jnp.where(right[s], my_rows[s], rows)
        return (at >= low) & (at < high)

    def outside(s, at):
        low = jnp.where(right[s], rows - far_rows[s], 0)
        high = jnp.where(right[s], rows, far_rows[s])
        return (at >= low) & (at < high)

    def within(t):
        return jnp.where(t < 0, 0, jnp.where(t > room - 1, room - 1, t))

    def split(t, per):
        slot = jnp.int32(0)
        for n in range(1, SLOTS):
            slot = slot + jnp.where(t >= n * per, 1, 0)
        return slot, t - slot * per

    operands = (qn, kn, vt, gt)

    def whole(ref, head):
        return ref[pl.ds(head * tiles, tiles)].reshape(rows, DH)

    out_slots = [[split(t, my_tiles[s]) for t in range(room)] for s in range(2)]
    back_slots = [[split(t, far_tiles[s]) for t in range(room)] for s in range(2)]

    def pack(s, g):
        for t in range(room):
            slot, at = out_slots[s][t]
            tile = my_base[s] + at
            tile = jnp.where(tile > tiles - 1, tiles - 1, tile)
            head = g * GROUP + jnp.where(right[s], GROUP - 1 - slot, slot)
            for a, ref in enumerate(operands):
                fwd_send[s, g, a, t] = ref[head * tiles + tile]

    def forward(s, g):
        return pltpu.make_async_remote_copy(
            fwd_send.at[s, g], fwd_recv[s][g], fwd_ss.at[s, g], fwd_rs.at[s, g], device_id={"seq": partner[s]}
        )

    def backward(s, g):
        return pltpu.make_async_remote_copy(
            ret_send.at[s, g], ret_recv[s][g], ret_ss.at[s, g], ret_rs.at[s, g], device_id={"seq": partner[s]}
        )

    for load in small[1:]:
        load.wait()
    for g in range(groups):
        for load in loads[g]:
            load.wait()
        for i in range(GROUP):
            head = g * GROUP + i
            for n, (src, dst, gain) in enumerate(((xq, qn, qgain_ref), (xk, kn, kgain_ref))):
                x = src[:, columns(head)].astype(jnp.float32)
                r = lax.rsqrt(jnp.mean(x * x, axis=1, keepdims=True) + EPSILON)
                normed = (x * r * gain[...]).astype(jnp.bfloat16)
                dst[pl.ds(head * tiles, tiles)] = normed.reshape(tiles, TILE, DH)
                rinv[n, head] = jnp.broadcast_to(r, (rows, DH))
            for src, dst in ((xv, vt), (xg, gt)):
                dst[pl.ds(head * tiles, tiles)] = src[:, columns(head)].reshape(tiles, TILE, DH)
        pack(0, g)
        if g == 0:
            pl.semaphore_wait(barrier, n_seq + n_dp - 2)
        for s in range(2):
            if s == 1:
                pack(1, g)

            @pl.when(exists[s])
            def _(s=s, g=g):
                forward(s, g).start()
    for d in range(1, n_dp):
        pl.semaphore_signal(ready, inc=1, device_id={"dp": lax.rem(my_dp + d, n_dp)})

    col = lax.broadcasted_iota(jnp.int32, (rows, 1), 0)
    row = lax.broadcasted_iota(jnp.int32, (1, rows), 1)
    start_col = jnp.zeros((rows, 1), jnp.int32)
    start_row = jnp.zeros((1, rows), jnp.int32)
    total = jnp.int32(0)
    for i in range(samples):
        total = total + len_ref[0, i]
        start_col = jnp.where(total <= col + first, total, start_col)
        start_row = jnp.where(total <= row + first, total, start_row)
    bias[2] = jnp.where(start_col == start_row, 0.0, MASKED)
    owned[2] = jnp.where(inside(0, row) | inside(1, row), 0.0, 1.0)
    square = lax.broadcasted_iota(jnp.int32, (rows, DH), 0)
    for s in range(2):
        valid_col = inside(s, col) | outside(s, col)
        valid_row = inside(s, row) | outside(s, row)
        bias[s] = jnp.where(valid_col, 0.0, MASKED) + jnp.where(valid_row, 0.0, MASKED)
        owned[s] = jnp.where(valid_row, 1.0, 0.0)
        mine[s] = jnp.where(inside(s, square), 1.0, 0.0).astype(jnp.bfloat16)
    gain_acc[...] = jnp.zeros_like(gain_acc)

    for s in range(2):
        @pl.when(jnp.logical_not(exists[s]))
        def _(s=s):
            for g in range(groups):
                fwd_recv[s][g][...] = jnp.zeros_like(fwd_recv[s][g])
                ret_recv[s][g][...] = jnp.zeros_like(ret_recv[s][g])

    rowrow = (((1,), (1,)), ((), ()))
    rowcol = (((1,), (0,)), ((), ()))
    colcol = (((0,), (0,)), ((), ()))
    dot = functools.partial(lax.dot_general, preferred_element_type=jnp.float32)

    def attend(blocks):
        scores = [dot(k, q, rowrow) * (factor * LOG2E) + bias_now for q, k, _, _, bias_now, _ in blocks]
        turned = [block[3].T for block in blocks]
        grad_weights = [dot(block[2], x, rowcol) for x, block in zip(turned, blocks)]
        highest = [jnp.max(x, axis=0, keepdims=True) for x in scores]
        powers = [jnp.exp2(x - y) for x, y in zip(scores, highest)]
        summed = [jnp.sum(x, axis=0, keepdims=True) for x in powers]
        weights = [x * (block[5] / y) for x, y, block in zip(powers, summed, blocks)]
        half_weights = [x.astype(jnp.bfloat16) for x in weights]
        attended = [dot(block[2], x, colcol) for x, block in zip(half_weights, blocks)]
        dv = [dot(x, block[3], rowcol) for x, block in zip(half_weights, blocks)]
        row_dot = [
            jnp.sum(x.astype(jnp.float32) * y.astype(jnp.bfloat16).astype(jnp.float32), axis=0, keepdims=True)
            for x, y in zip(turned, attended)
        ]
        grad_scores = [(x * (y - z)).astype(jnp.bfloat16) for x, y, z in zip(weights, grad_weights, row_dot)]
        dk = [dot(x, block[0], rowcol) for x, block in zip(grad_scores, blocks)]
        dq = [dot(x, block[1], colcol) for x, block in zip(grad_scores, blocks)]
        for n, totals in enumerate((dq, dk)):
            terms = sum(x * block[n].astype(jnp.float32) for x, block in zip(totals, blocks))
            gain_acc[n] += jnp.sum(terms.reshape(rows // 8, 8, DH), axis=0)
        return [tuple(x.astype(jnp.bfloat16) for x in result) for result in zip(dq, dk, dv)]

    batch = 2 * SLOTS if heads % (2 * SLOTS) == 0 else GROUP

    @pl.loop(0, heads // batch)
    def _(b):
        spots = [b * batch + i for i in range(batch)]
        results = attend([(*(whole(ref, head) for ref in operands), bias[2], owned[2]) for head in spots])
        for head, result in zip(spots, results):
            for a in range(3):
                local[a, :, columns(head)] = result[a]

    def crossing(s, g):
        own = mine[s] > 0.5
        found = []
        for i in range(SLOTS):
            head = g * GROUP + jnp.where(right[s], i, GROUP - 1 - i)
            there = [
                within(i * far_tiles[s] + t - far_base[s]) for t in range(tiles)
            ]
            parts = []
            for a, ref in enumerate(operands):
                other = jnp.concatenate([fwd_recv[s][g][a, t] for t in there], axis=0)
                parts.append(jnp.where(own, whole(ref, head), other))
            real = jnp.where(i < own_count[s], 1.0, 0.0)
            found.append((*parts, bias[s], owned[s] * real))
        return found

    def pack_back(s, g):
        for t in range(room):
            slot, at = back_slots[s][t]
            tile = far_base[s] + at
            tile = jnp.where(tile > tiles - 1, tiles - 1, tile)
            for a in range(3):
                ret_send[s, g, a, t] = stage[s, g, a, slot * tiles + tile]

    def cross(*parts):
        for s, g in parts:
            @pl.when(exists[s])
            def _(s=s, g=g):
                forward(s, g).wait_recv()
        results = attend([block for s, g in parts for block in crossing(s, g)])
        for n, (s, g) in enumerate(parts):
            for i in range(SLOTS):
                for a in range(3):
                    result = results[n * SLOTS + i][a]
                    stage[s, g, a, i * tiles:(i + 1) * tiles] = result.reshape(tiles, TILE, DH)

    def send_back(s, g):
        pack_back(s, g)

        @pl.when(exists[s])
        def _():
            backward(s, g).start()

    last = groups - 1
    inner = [(1, g) for g in range(last)]
    for parts in (inner, [(0, 0), (1, last)], *([(0, g)] for g in range(1, last))):
        cross(*parts)
        for part in parts:
            send_back(*part)
    cross((0, last))

    count = n_seq * n_dp
    place = my_dp * n_seq + me
    gains = (qgain_ref, kgain_ref)
    for n in range(2):
        all_gain[place, n:n + 1] = jnp.sum(gain_acc[n], axis=0, keepdims=True) * factor / gains[n][...]

    def share(d):
        to = lax.rem(place + d, count)
        return pltpu.make_async_remote_copy(
            all_gain.at[place], all_gain.at[place], gain_ss, gain_rs,
            device_id={"dp": lax.div(to, n_seq), "seq": lax.rem(to, n_seq)},
        )

    def share_all():
        others = all_gain.at[pl.ds(0, count - 1)]
        return pltpu.make_async_remote_copy(others, others, gain_ss, gain_rs, device_id={"seq": partner[1]})

    pl.semaphore_wait(ready, n_dp - 1)
    if count <= 64:
        for d in range(1, count):
            share(d).start()
    else:
        @pl.loop(1, count)
        def _(d):
            share(d).start()
    send_back(0, last)

    def merge(g):
        for s in range(2):
            @pl.when(exists[s])
            def _(s=s):
                backward(s, g).wait_recv()
        own_rows = [mine[s] > 0.5 for s in range(2)]
        for i in range(GROUP):
            head = g * GROUP + i
            cols = columns(head)
            merged = []
            for a in range(3):
                value = local[a, :, cols]
                for s in range(2):
                    slot = jnp.where(right[s], i, GROUP - 1 - i)
                    kept = stage[s, g, a, pl.ds(jnp.minimum(slot, SLOTS - 1) * tiles, tiles)].reshape(rows, DH)
                    there = [
                        within((GROUP - 1 - slot) * my_tiles[s] + t - my_base[s])
                        for t in range(tiles)
                    ]
                    back = jnp.concatenate([ret_recv[s][g][a, t] for t in there], axis=0)
                    ours = jnp.full((rows, DH), slot) < own_count[s]
                    chosen = jnp.where(ours, kept, back)
                    value = jnp.where(own_rows[s], chosen, value)
                merged.append(value)
            for n, (src, gain) in enumerate(((xq, qgain_ref), (xk, kgain_ref))):
                outputs[n][0, :, cols] = norm_back(
                    merged[n].astype(jnp.float32), src[:, cols].astype(jnp.float32), rinv[n, head], gain[...] * factor
                )
            dv_ref[0, :, cols] = merged[2]

    for g in range(groups):
        merge(g)
    share_all().wait_recv()
    gain_ref[...] = jnp.sum(all_gain[...], axis=0)
    share_all().wait_send()

    for s in range(2):
        @pl.when(exists[s])
        def _(s=s):
            for g in range(groups):
                forward(s, g).wait_send()
                backward(s, g).wait_send()


def write_back(dq_in, dk_in, dv_in, gain_in, dq_ref, dk_ref, dv_ref, gain_ref, sem):
    copies = [
        pltpu.make_async_copy(held, out, sem.at[i])
        for i, (held, out) in enumerate(
            ((dq_in, dq_ref), (dk_in, dk_ref), (dv_in, dv_ref), (gain_in, gain_ref))
        )
    ]
    for copy in copies:
        copy.start()
    for copy in copies:
        copy.wait()


def body(query_rows, key_rows, value_rows, out_grad, query_gain, key_gain, lengths):
    rows, width = query_rows.shape[1:]
    samples = lengths.shape[1]
    n_seq, n_dp = lax.axis_size("seq"), lax.axis_size("dp")
    heads = width // DH
    groups = heads // GROUP
    counts, room = division(rows // TILE)
    big = jax.ShapeDtypeStruct((1, rows, width), jnp.bfloat16)
    anywhere = pl.BlockSpec(memory_space=pl.ANY)
    hbm = pl.BlockSpec(memory_space=pltpu.HBM)
    vmem = pl.BlockSpec(memory_space=pltpu.VMEM)
    dma = pltpu.SemaphoreType.DMA
    half = jnp.bfloat16
    limit = 67043328 - 3 * big.size * 2 - 131072
    shapes = (big, big, big, jax.ShapeDtypeStruct((2, DH), jnp.float32))
    results = pl.pallas_call(
        functools.partial(kernel, rows, width, samples, n_seq, n_dp, room, counts),
        out_shape=tuple(pltpu.VMEM(x.shape, x.dtype) for x in shapes),
        in_specs=[hbm] * 4 + [hbm] * 3,
        out_specs=(vmem, vmem, vmem, vmem),
        scratch_shapes=[
            pltpu.VMEM((1, DH), jnp.float32),
            pltpu.VMEM((1, DH), jnp.float32),
            pltpu.SMEM((1, samples), jnp.int32),
            *[pltpu.VMEM((rows, width), half)] * 4,
            *[pltpu.VMEM((heads * rows // TILE, TILE, DH), half)] * 4,
            pltpu.VMEM((2, heads, rows, DH), jnp.float32),
            pltpu.VMEM((3, rows, width), half),
            pltpu.VMEM((3, rows, rows), jnp.float32),
            pltpu.VMEM((3, 1, rows), jnp.float32),
            pltpu.VMEM((2, rows, DH), half),
            pltpu.VMEM((2, groups, 4, room, TILE, DH), half),
            pltpu.VMEM((2, groups, 3, room, TILE, DH), half),
            pltpu.VMEM((2, groups, 3, SLOTS * rows // TILE, TILE, DH), half),
            pltpu.VMEM((2, 8, DH), jnp.float32),
            pltpu.VMEM((n_seq * n_dp, 2, DH), jnp.float32),
            *[pltpu.VMEM((4, room, TILE, DH), half)] * (2 * groups),
            *[pltpu.VMEM((3, room, TILE, DH), half)] * (2 * groups),
            dma((groups + 1, 4)),
            dma((2, groups)),
            dma((2, groups)),
            dma((2, groups)),
            dma((2, groups)),
            dma(()),
            dma(()),
            pltpu.SemaphoreType.REGULAR,
        ],
        compiler_params=pltpu.CompilerParams(collective_id=0, has_side_effects=True, vmem_limit_bytes=limit),
    )(
        query_rows, key_rows, value_rows, out_grad,
        query_gain.reshape(1, DH), key_gain.reshape(1, DH), lengths,
    )
    return pl.pallas_call(
        write_back,
        out_shape=shapes,
        in_specs=[anywhere] * 4,
        out_specs=(anywhere,) * 4,
        scratch_shapes=[dma((4,))],
        compiler_params=pltpu.CompilerParams(vmem_limit_bytes=8 << 20),
    )(*results)


def solution(mesh):
    placed = (
        P("dp", "seq", None),
        P("dp", "seq", None),
        P("dp", "seq", None),
        P("dp", "seq", None),
        P(),
        P(),
        P("dp", None),
    )
    return jax.shard_map(
        body,
        mesh=mesh,
        in_specs=placed,
        out_specs=(P("dp", "seq", None), P("dp", "seq", None), P("dp", "seq", None), P()),
        check_vma=False,
    )
```

```python
import functools

import jax
import jax.numpy as jnp
from jax import lax
from jax.experimental import pallas as pl
from jax.experimental.pallas import tpu as pltpu
from jax.sharding import PartitionSpec as P

DH = 128
EPSILON = 1e-06
MASKED = -1e30
TILE = 16
GROUP = 4
SLOTS = GROUP - 1
LOG2E = 1.4426950408889634


def division(tiles):
    counts, most = [SLOTS], 0
    for left in range(1, tiles + 1):
        right = tiles + 1 - left
        need, taken = min((max(t * left, (GROUP - t) * right), -t) for t in range(1, GROUP))
        counts.append(-taken)
        most = max(most, need)
    return counts, most


def norm_back(grad, rows_in, inverse, gain):
    unit = rows_in * inverse
    scaled = grad * gain
    inner = jnp.mean(scaled * unit, axis=1, keepdims=True)
    return (inverse * (scaled - unit * inner)).astype(jnp.bfloat16)


def kernel(rows, width, samples, n_seq, n_dp, room, counts, *refs):
    heads = width // DH
    groups = heads // GROUP
    tiles = rows // TILE
    factor = DH ** (-0.5)
    refs = list(refs)

    def take(n):
        got = refs[:n]
        del refs[:n]
        return got

    q_in, k_in, v_in, g_in, qgain_in, kgain_in, len_in = take(7)
    dq_ref, dk_ref, dv_ref, gain_ref = take(4)
    qgain_ref, kgain_ref, len_ref = take(3)
    xq, xk, xv, xg, qn, kn, vt, gt, rinv, local, bias, owned, mine = take(13)
    fwd_send, ret_send, stage, gain_acc, all_gain = take(5)
    fwd_recv = [take(groups) for _ in range(2)]
    ret_recv = [take(groups) for _ in range(2)]
    (load_sem, fwd_ss, fwd_rs, ret_ss, ret_rs, gain_ss, gain_rs, here, lines, ready) = take(10)

    me = lax.axis_index("seq")
    my_dp = lax.axis_index("dp")
    odd = lax.rem(me, 2)
    outputs = (dq_ref, dk_ref, dv_ref)

    right = (odd == 0, odd == 1)
    partner = (jnp.where(odd == 0, me - 1, me + 1), jnp.where(odd == 0, me + 1, me - 1))
    exists = tuple((p >= 0) & (p < n_seq) for p in partner)

    def columns(head):
        return pl.ds(pl.multiple_of(head * DH, DH), DH)

    def span(g):
        return pl.ds(g * GROUP * DH, GROUP * DH)

    small = [
        pltpu.make_async_copy(src, dst, load_sem.at[groups, i])
        for i, (src, dst) in enumerate(((len_in, len_ref), (qgain_in, qgain_ref), (kgain_in, kgain_ref)))
    ]
    loads = [
        [
            pltpu.make_async_copy(src.at[0, :, span(g)], dst.at[:, span(g)], load_sem.at[g, i])
            for i, (src, dst) in enumerate(((q_in, xq), (k_in, xk), (v_in, xv), (g_in, xg)))
        ]
        for g in range(groups)
    ]

    barrier = pltpu.get_barrier_semaphore()
    for s in range(2):
        @pl.when(exists[s])
        def _(s=s):
            pl.semaphore_signal(barrier, inc=1, device_id={"seq": partner[s]})
    small[0].start()
    for load in loads[0]:
        load.start()
    head_of_line = me == 0

    @pl.when(head_of_line)
    def _():
        for d in range(1, n_dp):
            pl.semaphore_signal(barrier, inc=1, device_id={"dp": lax.rem(my_dp + d, n_dp)})
        for d in range(2, n_seq):
            pl.semaphore_signal(barrier, inc=1, device_id={"seq": d})

    expected = jnp.where(head_of_line, n_dp - 1, jnp.where(me >= 2, 1, 0))
    expected = expected + jnp.where(exists[0], 1, 0) + jnp.where(exists[1], 1, 0)
    for load in small[1:]:
        load.start()
    for g in range(1, groups):
        for load in loads[g]:
            load.start()
    small[0].wait()

    far = rows * n_seq + 2 * rows
    first = me * rows

    edge = [jnp.where(right[s], first, first + rows) for s in range(2)]
    start = [jnp.int32(0), jnp.int32(0)]
    end = [jnp.int32(far), jnp.int32(far)]
    total = jnp.int32(0)
    for i in range(samples):
        total = total + len_ref[0, i]
        for s in range(2):
            end[s] = jnp.where(total > edge[s], jnp.minimum(end[s], total), end[s])
            start[s] = jnp.where(total <= edge[s], total, start[s])

    def tile_count(n):
        return sum(jnp.where(n > t * TILE, 1, 0) for t in range(tiles))

    my_rows, far_rows, my_tiles, far_tiles, my_base, far_base, own_count = [], [], [], [], [], [], []
    for s in range(2):
        before = edge[s] - start[s]
        after = jnp.where(before > 0, end[s] - edge[s], 0)
        mr = jnp.where(right[s], after, before)
        fr = jnp.where(right[s], before, after)
        mt = tile_count(mr)
        ft = tile_count(fr)
        lt = jnp.where(right[s], ft, mt)
        taken = jnp.int32(counts[0])
        for n in range(1, len(counts)):
            if counts[n] != counts[n - 1]:
                taken = jnp.where(lt >= n, counts[n], taken)
        my_rows.append(mr)
        far_rows.append(fr)
        my_tiles.append(mt)
        far_tiles.append(ft)
        my_base.append(jnp.where(right[s], 0, tiles - mt))
        far_base.append(jnp.where(right[s], tiles - ft, 0))
        own_count.append(jnp.where(right[s], taken, GROUP - taken))

    def inside(s, at):
        low = jnp.where(right[s], 0, rows - my_rows[s])
        high = jnp.where(right[s], my_rows[s], rows)
        return (at >= low) & (at < high)

    def outside(s, at):
        low = jnp.where(right[s], rows - far_rows[s], 0)
        high = jnp.where(right[s], rows, far_rows[s])
        return (at >= low) & (at < high)

    def within(t):
        return jnp.where(t < 0, 0, jnp.where(t > room - 1, room - 1, t))

    def split(t, per):
        slot = jnp.int32(0)
        for n in range(1, SLOTS):
            slot = slot + jnp.where(t >= n * per, 1, 0)
        return slot, t - slot * per

    operands = (qn, kn, vt, gt)

    def whole(ref, head):
        return ref[pl.ds(head * tiles, tiles)].reshape(rows, DH)

    out_slots = [[split(t, my_tiles[s]) for t in range(room)] for s in range(2)]
    back_slots = [[split(t, far_tiles[s]) for t in range(room)] for s in range(2)]

    def pack(s, g):
        for t in range(room):
            slot, at = out_slots[s][t]
            tile = my_base[s] + at
            tile = jnp.where(tile > tiles - 1, tiles - 1, tile)
            head = g * GROUP + jnp.where(right[s], GROUP - 1 - slot, slot)
            for a, ref in enumerate(operands):
                fwd_send[s, g, a, t] = ref[head * tiles + tile]

    def forward(s, g):
        return pltpu.make_async_remote_copy(
            fwd_send.at[s, g], fwd_recv[s][g], fwd_ss.at[s, g], fwd_rs.at[s, g], device_id={"seq": partner[s]}
        )

    def backward(s, g):
        return pltpu.make_async_remote_copy(
            ret_send.at[s, g], ret_recv[s][g], ret_ss.at[s, g], ret_rs.at[s, g], device_id={"seq": partner[s]}
        )

    for load in small[1:]:
        load.wait()
    for g in range(groups):
        for load in loads[g]:
            load.wait()
        for i in range(GROUP):
            head = g * GROUP + i
            for n, (src, dst, gain) in enumerate(((xq, qn, qgain_ref), (xk, kn, kgain_ref))):
                x = src[:, columns(head)].astype(jnp.float32)
                r = lax.rsqrt(jnp.mean(x * x, axis=1, keepdims=True) + EPSILON)
                normed = (x * r * gain[...]).astype(jnp.bfloat16)
                dst[pl.ds(head * tiles, tiles)] = normed.reshape(tiles, TILE, DH)
                rinv[n, head] = jnp.broadcast_to(r, (rows, DH))
            for src, dst in ((xv, vt), (xg, gt)):
                dst[pl.ds(head * tiles, tiles)] = src[:, columns(head)].reshape(tiles, TILE, DH)
        pack(0, g)
        if g == 0:
            pl.semaphore_wait(barrier, expected)
        for s in range(2):
            if s == 1:
                pack(1, g)

            @pl.when(exists[s])
            def _(s=s, g=g):
                forward(s, g).start()
            if (g, s) == (0, 0):
                @pl.when(me > 0)
                def _():
                    pl.semaphore_signal(here, inc=1, device_id={"seq": 0})
    col = lax.broadcasted_iota(jnp.int32, (rows, 1), 0)
    row = lax.broadcasted_iota(jnp.int32, (1, rows), 1)
    start_col = jnp.zeros((rows, 1), jnp.int32)
    start_row = jnp.zeros((1, rows), jnp.int32)
    total = jnp.int32(0)
    for i in range(samples):
        total = total + len_ref[0, i]
        start_col = jnp.where(total <= col + first, total, start_col)
        start_row = jnp.where(total <= row + first, total, start_row)
    bias[2] = jnp.where(start_col == start_row, 0.0, MASKED)
    owned[2] = jnp.where(inside(0, row) | inside(1, row), 0.0, 1.0)
    square = lax.broadcasted_iota(jnp.int32, (rows, DH), 0)
    for s in range(2):
        valid_col = inside(s, col) | outside(s, col)
        valid_row = inside(s, row) | outside(s, row)
        bias[s] = jnp.where(valid_col, 0.0, MASKED) + jnp.where(valid_row, 0.0, MASKED)
        owned[s] = jnp.where(valid_row, 1.0, 0.0)
        mine[s] = jnp.where(inside(s, square), 1.0, 0.0).astype(jnp.bfloat16)
    gain_acc[...] = jnp.zeros_like(gain_acc)

    for s in range(2):
        @pl.when(jnp.logical_not(exists[s]))
        def _(s=s):
            for g in range(groups):
                fwd_recv[s][g][...] = jnp.zeros_like(fwd_recv[s][g])
                ret_recv[s][g][...] = jnp.zeros_like(ret_recv[s][g])

    rowrow = (((1,), (1,)), ((), ()))
    rowcol = (((1,), (0,)), ((), ()))
    colcol = (((0,), (0,)), ((), ()))
    dot = functools.partial(lax.dot_general, preferred_element_type=jnp.float32)

    def attend(blocks):
        scores = [dot(k, q, rowrow) * (factor * LOG2E) + bias_now for q, k, _, _, bias_now, _ in blocks]
        turned = [block[3].T for block in blocks]
        grad_weights = [dot(block[2], x, rowcol) for x, block in zip(turned, blocks)]
        highest = [jnp.max(x, axis=0, keepdims=True) for x in scores]
        powers = [jnp.exp2(x - y) for x, y in zip(scores, highest)]
        summed = [jnp.sum(x, axis=0, keepdims=True) for x in powers]
        weights = [x * (block[5] / y) for x, y, block in zip(powers, summed, blocks)]
        half_weights = [x.astype(jnp.bfloat16) for x in weights]
        attended = [dot(block[2], x, colcol) for x, block in zip(half_weights, blocks)]
        dv = [dot(x, block[3], rowcol) for x, block in zip(half_weights, blocks)]
        row_dot = [
            jnp.sum(x.astype(jnp.float32) * y.astype(jnp.bfloat16).astype(jnp.float32), axis=0, keepdims=True)
            for x, y in zip(turned, attended)
        ]
        grad_scores = [(x * (y - z)).astype(jnp.bfloat16) for x, y, z in zip(weights, grad_weights, row_dot)]
        dk = [dot(x, block[0], rowcol) for x, block in zip(grad_scores, blocks)]
        dq = [dot(x, block[1], colcol) for x, block in zip(grad_scores, blocks)]
        for n, totals in enumerate((dq, dk)):
            terms = sum(x * block[n].astype(jnp.float32) for x, block in zip(totals, blocks))
            gain_acc[n] += jnp.sum(terms.reshape(rows // 8, 8, DH), axis=0)
        return [tuple(x.astype(jnp.bfloat16) for x in result) for result in zip(dq, dk, dv)]

    batch = 2 * SLOTS if heads % (2 * SLOTS) == 0 else GROUP

    @pl.loop(0, heads // batch)
    def _(b):
        spots = [b * batch + i for i in range(batch)]
        results = attend([(*(whole(ref, head) for ref in operands), bias[2], owned[2]) for head in spots])
        for head, result in zip(spots, results):
            for a in range(3):
                local[a, :, columns(head)] = result[a]

    def crossing(s, g):
        own = mine[s] > 0.5
        found = []
        for i in range(SLOTS):
            head = g * GROUP + jnp.where(right[s], i, GROUP - 1 - i)
            there = [
                within(i * far_tiles[s] + t - far_base[s]) for t in range(tiles)
            ]
            parts = []
            for a, ref in enumerate(operands):
                other = jnp.concatenate([fwd_recv[s][g][a, t] for t in there], axis=0)
                parts.append(jnp.where(own, whole(ref, head), other))
            real = jnp.where(i < own_count[s], 1.0, 0.0)
            found.append((*parts, bias[s], owned[s] * real))
        return found

    def pack_back(s, g):
        for t in range(room):
            slot, at = back_slots[s][t]
            tile = far_base[s] + at
            tile = jnp.where(tile > tiles - 1, tiles - 1, tile)
            for a in range(3):
                ret_send[s, g, a, t] = stage[s, g, a, slot * tiles + tile]

    def cross(*parts):
        for s, g in parts:
            @pl.when(exists[s])
            def _(s=s, g=g):
                forward(s, g).wait_recv()
        results = attend([block for s, g in parts for block in crossing(s, g)])
        for n, (s, g) in enumerate(parts):
            for i in range(SLOTS):
                for a in range(3):
                    result = results[n * SLOTS + i][a]
                    stage[s, g, a, i * tiles:(i + 1) * tiles] = result.reshape(tiles, TILE, DH)

    def send_back(s, g):
        pack_back(s, g)

        @pl.when(exists[s])
        def _():
            backward(s, g).start()

    @pl.when(head_of_line)
    def _():
        pl.semaphore_wait(here, n_seq - 1)
        for d in range(1, n_dp):
            pl.semaphore_signal(lines, inc=1, device_id={"dp": lax.rem(my_dp + d, n_dp)})

    last = groups - 1
    inner = [(1, g) for g in range(last)]
    for parts in (inner, [(1, last)], *([(0, g)] for g in range(last))):
        cross(*parts)
        for part in parts:
            if part != (0, last - 1):
                send_back(*part)
        if parts == inner:
            @pl.when(head_of_line)
            def _():
                pl.semaphore_wait(lines, n_dp - 1)
                for d in range(1, n_seq):
                    pl.semaphore_signal(ready, inc=1, device_id={"seq": d})
    cross((0, last))

    count = n_seq * n_dp
    place = my_dp * n_seq + me
    gains = (qgain_ref, kgain_ref)
    for n in range(2):
        all_gain[place, n:n + 1] = jnp.sum(gain_acc[n], axis=0, keepdims=True) * factor / gains[n][...]

    def share(dp, seq):
        return pltpu.make_async_remote_copy(
            all_gain.at[place], all_gain.at[place], gain_ss, gain_rs, device_id={"dp": dp, "seq": seq}
        )

    def share_with(seq):
        for d in range(1, n_dp):
            share(lax.rem(my_dp + d, n_dp), seq).start()

    def share_all():
        others = all_gain.at[pl.ds(0, count - 1)]
        return pltpu.make_async_remote_copy(others, others, gain_ss, gain_rs, device_id={"seq": partner[1]})

    @pl.when(me > 0)
    def _():
        pl.semaphore_wait(ready, 1)

    if count <= 64:
        for n in range(n_seq):
            share_with(n)
            if n > 0:
                share(my_dp, lax.rem(me + n, n_seq)).start()
    else:
        @pl.loop(0, n_seq)
        def _(n):
            share_with(n)

        @pl.loop(1, n_seq)
        def _(n):
            share(my_dp, lax.rem(me + n, n_seq)).start()
    send_back(0, last - 1)
    send_back(0, last)

    def merge(g):
        for s in range(2):
            @pl.when(exists[s])
            def _(s=s):
                backward(s, g).wait_recv()
        own_rows = [mine[s] > 0.5 for s in range(2)]
        for i in range(GROUP):
            head = g * GROUP + i
            cols = columns(head)
            merged = []
            for a in range(3):
                value = local[a, :, cols]
                for s in range(2):
                    slot = jnp.where(right[s], i, GROUP - 1 - i)
                    kept = stage[s, g, a, pl.ds(jnp.minimum(slot, SLOTS - 1) * tiles, tiles)].reshape(rows, DH)
                    there = [
                        within((GROUP - 1 - slot) * my_tiles[s] + t - my_base[s])
                        for t in range(tiles)
                    ]
                    back = jnp.concatenate([ret_recv[s][g][a, t] for t in there], axis=0)
                    ours = jnp.full((rows, DH), slot) < own_count[s]
                    chosen = jnp.where(ours, kept, back)
                    value = jnp.where(own_rows[s], chosen, value)
                merged.append(value)
            for n, (src, gain) in enumerate(((xq, qgain_ref), (xk, kgain_ref))):
                outputs[n][0, :, cols] = norm_back(
                    merged[n].astype(jnp.float32), src[:, cols].astype(jnp.float32), rinv[n, head], gain[...] * factor
                )
            dv_ref[0, :, cols] = merged[2]

    for g in range(groups):
        merge(g)
    share_all().wait_recv()
    gain_ref[...] = jnp.sum(all_gain[...], axis=0)
    share_all().wait_send()

    for s in range(2):
        @pl.when(exists[s])
        def _(s=s):
            for g in range(groups):
                forward(s, g).wait_send()
                backward(s, g).wait_send()


def write_back(dq_in, dk_in, dv_in, gain_in, dq_ref, dk_ref, dv_ref, gain_ref, sem):
    copies = [
        pltpu.make_async_copy(held, out, sem.at[i])
        for i, (held, out) in enumerate(
            ((dq_in, dq_ref), (dk_in, dk_ref), (dv_in, dv_ref), (gain_in, gain_ref))
        )
    ]
    for copy in copies:
        copy.start()
    for copy in copies:
        copy.wait()


def body(query_rows, key_rows, value_rows, out_grad, query_gain, key_gain, lengths):
    rows, width = query_rows.shape[1:]
    samples = lengths.shape[1]
    n_seq, n_dp = lax.axis_size("seq"), lax.axis_size("dp")
    heads = width // DH
    groups = heads // GROUP
    counts, room = division(rows // TILE)
    big = jax.ShapeDtypeStruct((1, rows, width), jnp.bfloat16)
    anywhere = pl.BlockSpec(memory_space=pl.ANY)
    hbm = pl.BlockSpec(memory_space=pltpu.HBM)
    vmem = pl.BlockSpec(memory_space=pltpu.VMEM)
    dma = pltpu.SemaphoreType.DMA
    half = jnp.bfloat16
    limit = 67043328 - 3 * big.size * 2 - 131072
    shapes = (big, big, big, jax.ShapeDtypeStruct((2, DH), jnp.float32))
    results = pl.pallas_call(
        functools.partial(kernel, rows, width, samples, n_seq, n_dp, room, counts),
        out_shape=tuple(pltpu.VMEM(x.shape, x.dtype) for x in shapes),
        in_specs=[hbm] * 4 + [hbm] * 3,
        out_specs=(vmem, vmem, vmem, vmem),
        scratch_shapes=[
            pltpu.VMEM((1, DH), jnp.float32),
            pltpu.VMEM((1, DH), jnp.float32),
            pltpu.SMEM((1, samples), jnp.int32),
            *[pltpu.VMEM((rows, width), half)] * 4,
            *[pltpu.VMEM((heads * rows // TILE, TILE, DH), half)] * 4,
            pltpu.VMEM((2, heads, rows, DH), jnp.float32),
            pltpu.VMEM((3, rows, width), half),
            pltpu.VMEM((3, rows, rows), jnp.float32),
            pltpu.VMEM((3, 1, rows), jnp.float32),
            pltpu.VMEM((2, rows, DH), half),
            pltpu.VMEM((2, groups, 4, room, TILE, DH), half),
            pltpu.VMEM((2, groups, 3, room, TILE, DH), half),
            pltpu.VMEM((2, groups, 3, SLOTS * rows // TILE, TILE, DH), half),
            pltpu.VMEM((2, 8, DH), jnp.float32),
            pltpu.VMEM((n_seq * n_dp, 2, DH), jnp.float32),
            *[pltpu.VMEM((4, room, TILE, DH), half)] * (2 * groups),
            *[pltpu.VMEM((3, room, TILE, DH), half)] * (2 * groups),
            dma((groups + 1, 4)),
            dma((2, groups)),
            dma((2, groups)),
            dma((2, groups)),
            dma((2, groups)),
            dma(()),
            dma(()),
            *[pltpu.SemaphoreType.REGULAR] * 3,
        ],
        compiler_params=pltpu.CompilerParams(collective_id=0, has_side_effects=True, vmem_limit_bytes=limit),
    )(
        query_rows, key_rows, value_rows, out_grad,
        query_gain.reshape(1, DH), key_gain.reshape(1, DH), lengths,
    )
    return pl.pallas_call(
        write_back,
        out_shape=shapes,
        in_specs=[anywhere] * 4,
        out_specs=(anywhere,) * 4,
        scratch_shapes=[dma((4,))],
        compiler_params=pltpu.CompilerParams(vmem_limit_bytes=8 << 20),
    )(*results)


def solution(mesh):
    placed = (
        P("dp", "seq", None),
        P("dp", "seq", None),
        P("dp", "seq", None),
        P("dp", "seq", None),
        P(),
        P(),
        P("dp", None),
    )
    return jax.shard_map(
        body,
        mesh=mesh,
        in_specs=placed,
        out_specs=(P("dp", "seq", None), P("dp", "seq", None), P("dp", "seq", None), P()),
        check_vma=False,
    )
```

```python
import functools

import jax
import jax.numpy as jnp
from jax import lax
from jax.experimental import pallas as pl
from jax.experimental.pallas import tpu as pltpu
from jax.sharding import PartitionSpec as P

DH = 128
EPSILON = 1e-06
MASKED = -1e30
TILE = 16
GROUP = 4
SLOTS = GROUP - 1
LOG2E = 1.4426950408889634


def division(tiles):
    counts, most = [SLOTS], 0
    for left in range(1, tiles + 1):
        right = tiles + 1 - left
        need, taken = min((max(t * left, (GROUP - t) * right), -t) for t in range(1, GROUP))
        counts.append(-taken)
        most = max(most, need)
    return counts, most


def norm_back(grad, rows_in, inverse, gain):
    unit = rows_in * inverse
    scaled = grad * gain
    inner = jnp.mean(scaled * unit, axis=1, keepdims=True)
    return (inverse * (scaled - unit * inner)).astype(jnp.bfloat16)


def kernel(rows, width, samples, n_seq, n_dp, room, counts, *refs):
    heads = width // DH
    groups = heads // GROUP
    tiles = rows // TILE
    factor = DH ** (-0.5)
    refs = list(refs)

    def take(n):
        got = refs[:n]
        del refs[:n]
        return got

    q_in, k_in, v_in, g_in, qgain_in, kgain_in, len_in = take(7)
    dq_ref, dk_ref, dv_ref, gain_ref = take(4)
    qgain_ref, kgain_ref, len_ref = take(3)
    xq, xk, xv, xg, qn, kn, vt, gt, rinv, local, bias, owned, mine = take(13)
    fwd_send, ret_send, stage, gain_acc, all_gain = take(5)
    fwd_recv = [take(groups) for _ in range(2)]
    ret_recv = [take(groups) for _ in range(2)]
    (load_sem, fwd_ss, fwd_rs, ret_ss, ret_rs, gain_ss, gain_rs, here, lines, ready) = take(10)

    me = lax.axis_index("seq")
    my_dp = lax.axis_index("dp")
    odd = lax.rem(me, 2)
    outputs = (dq_ref, dk_ref, dv_ref)

    right = (odd == 0, odd == 1)
    partner = (jnp.where(odd == 0, me - 1, me + 1), jnp.where(odd == 0, me + 1, me - 1))
    exists = tuple((p >= 0) & (p < n_seq) for p in partner)

    def columns(head):
        return pl.ds(pl.multiple_of(head * DH, DH), DH)

    def span(g):
        return pl.ds(g * GROUP * DH, GROUP * DH)

    small = [
        pltpu.make_async_copy(src, dst, load_sem.at[groups, i])
        for i, (src, dst) in enumerate(((len_in, len_ref), (qgain_in, qgain_ref), (kgain_in, kgain_ref)))
    ]
    loads = [
        [
            pltpu.make_async_copy(src.at[0, :, span(g)], dst.at[:, span(g)], load_sem.at[g, i])
            for i, (src, dst) in enumerate(((q_in, xq), (k_in, xk), (v_in, xv), (g_in, xg)))
        ]
        for g in range(groups)
    ]

    barrier = pltpu.get_barrier_semaphore()
    for s in range(2):
        @pl.when(exists[s])
        def _(s=s):
            pl.semaphore_signal(barrier, inc=1, device_id={"seq": partner[s]})
    small[0].start()
    for load in loads[0]:
        load.start()
    head_of_line = me == 0

    @pl.when(head_of_line)
    def _():
        for d in range(1, n_dp):
            pl.semaphore_signal(barrier, inc=1, device_id={"dp": lax.rem(my_dp + d, n_dp)})
        for d in range(2, n_seq):
            pl.semaphore_signal(barrier, inc=1, device_id={"seq": d})

    expected = jnp.where(head_of_line, n_dp - 1, jnp.where(me >= 2, 1, 0))
    expected = expected + jnp.where(exists[0], 1, 0) + jnp.where(exists[1], 1, 0)
    for load in small[1:]:
        load.start()
    for g in range(1, groups):
        for load in loads[g]:
            load.start()
    small[0].wait()

    far = rows * n_seq + 2 * rows
    first = me * rows

    edge = [jnp.where(right[s], first, first + rows) for s in range(2)]
    start = [jnp.int32(0), jnp.int32(0)]
    end = [jnp.int32(far), jnp.int32(far)]
    total = jnp.int32(0)
    for i in range(samples):
        total = total + len_ref[0, i]
        for s in range(2):
            end[s] = jnp.where(total > edge[s], jnp.minimum(end[s], total), end[s])
            start[s] = jnp.where(total <= edge[s], total, start[s])

    def tile_count(n):
        return sum(jnp.where(n > t * TILE, 1, 0) for t in range(tiles))

    my_rows, far_rows, my_tiles, far_tiles, my_base, far_base, own_count = [], [], [], [], [], [], []
    for s in range(2):
        before = edge[s] - start[s]
        after = jnp.where(before > 0, end[s] - edge[s], 0)
        mr = jnp.where(right[s], after, before)
        fr = jnp.where(right[s], before, after)
        mt = tile_count(mr)
        ft = tile_count(fr)
        lt = jnp.where(right[s], ft, mt)
        taken = jnp.int32(counts[0])
        for n in range(1, len(counts)):
            if counts[n] != counts[n - 1]:
                taken = jnp.where(lt >= n, counts[n], taken)
        my_rows.append(mr)
        far_rows.append(fr)
        my_tiles.append(mt)
        far_tiles.append(ft)
        my_base.append(jnp.where(right[s], 0, tiles - mt))
        far_base.append(jnp.where(right[s], tiles - ft, 0))
        own_count.append(jnp.where(right[s], taken, GROUP - taken))

    def inside(s, at):
        low = jnp.where(right[s], 0, rows - my_rows[s])
        high = jnp.where(right[s], my_rows[s], rows)
        return (at >= low) & (at < high)

    def outside(s, at):
        low = jnp.where(right[s], rows - far_rows[s], 0)
        high = jnp.where(right[s], rows, far_rows[s])
        return (at >= low) & (at < high)

    def within(t):
        return jnp.where(t < 0, 0, jnp.where(t > room - 1, room - 1, t))

    def split(t, per):
        slot = jnp.int32(0)
        for n in range(1, SLOTS):
            slot = slot + jnp.where(t >= n * per, 1, 0)
        return slot, t - slot * per

    operands = (qn, kn, vt, gt)

    def whole(ref, head):
        return ref[pl.ds(head * tiles, tiles)].reshape(rows, DH)

    out_slots = [[split(t, my_tiles[s]) for t in range(room)] for s in range(2)]
    back_slots = [[split(t, far_tiles[s]) for t in range(room)] for s in range(2)]

    def pack(s, g):
        for t in range(room):
            slot, at = out_slots[s][t]
            tile = my_base[s] + at
            tile = jnp.where(tile > tiles - 1, tiles - 1, tile)
            head = g * GROUP + jnp.where(right[s], GROUP - 1 - slot, slot)
            for a, ref in enumerate(operands):
                fwd_send[s, g, a, t] = ref[head * tiles + tile]

    def forward(s, g):
        return pltpu.make_async_remote_copy(
            fwd_send.at[s, g], fwd_recv[s][g], fwd_ss.at[s, g], fwd_rs.at[s, g], device_id={"seq": partner[s]}
        )

    def backward(s, g):
        return pltpu.make_async_remote_copy(
            ret_send.at[s, g], ret_recv[s][g], ret_ss.at[s, g], ret_rs.at[s, g], device_id={"seq": partner[s]}
        )

    for load in small[1:]:
        load.wait()
    for g in range(groups):
        for load in loads[g]:
            load.wait()
        for i in range(GROUP):
            head = g * GROUP + i
            for n, (src, dst, gain) in enumerate(((xq, qn, qgain_ref), (xk, kn, kgain_ref))):
                x = src[:, columns(head)].astype(jnp.float32)
                r = lax.rsqrt(jnp.mean(x * x, axis=1, keepdims=True) + EPSILON)
                normed = (x * r * gain[...]).astype(jnp.bfloat16)
                dst[pl.ds(head * tiles, tiles)] = normed.reshape(tiles, TILE, DH)
                rinv[n, head] = jnp.broadcast_to(r, (rows, DH))
            for src, dst in ((xv, vt), (xg, gt)):
                dst[pl.ds(head * tiles, tiles)] = src[:, columns(head)].reshape(tiles, TILE, DH)
        pack(0, g)
        if g == 0:
            pl.semaphore_wait(barrier, expected)
        for s in range(2):
            if s == 1:
                pack(1, g)

            @pl.when(exists[s])
            def _(s=s, g=g):
                forward(s, g).start()
            if (g, s) == (0, 0):
                @pl.when(me > 0)
                def _():
                    pl.semaphore_signal(here, inc=1, device_id={"seq": 0})
    col = lax.broadcasted_iota(jnp.int32, (rows, 1), 0)
    row = lax.broadcasted_iota(jnp.int32, (1, rows), 1)
    start_col = jnp.zeros((rows, 1), jnp.int32)
    start_row = jnp.zeros((1, rows), jnp.int32)
    total = jnp.int32(0)
    for i in range(samples):
        total = total + len_ref[0, i]
        start_col = jnp.where(total <= col + first, total, start_col)
        start_row = jnp.where(total <= row + first, total, start_row)
    bias[2] = jnp.where(start_col == start_row, 0.0, MASKED)
    owned[2] = jnp.where(inside(0, row) | inside(1, row), 0.0, 1.0)
    square = lax.broadcasted_iota(jnp.int32, (rows, DH), 0)
    for s in range(2):
        valid_col = inside(s, col) | outside(s, col)
        valid_row = inside(s, row) | outside(s, row)
        bias[s] = jnp.where(valid_col, 0.0, MASKED) + jnp.where(valid_row, 0.0, MASKED)
        owned[s] = jnp.where(valid_row, 1.0, 0.0)
        mine[s] = jnp.where(inside(s, square), 1.0, 0.0).astype(jnp.bfloat16)
    gain_acc[...] = jnp.zeros_like(gain_acc)

    for s in range(2):
        @pl.when(jnp.logical_not(exists[s]))
        def _(s=s):
            for g in range(groups):
                fwd_recv[s][g][...] = jnp.zeros_like(fwd_recv[s][g])
                ret_recv[s][g][...] = jnp.zeros_like(ret_recv[s][g])

    rowrow = (((1,), (1,)), ((), ()))
    rowcol = (((1,), (0,)), ((), ()))
    colcol = (((0,), (0,)), ((), ()))
    dot = functools.partial(lax.dot_general, preferred_element_type=jnp.float32)

    def attend(blocks):
        scores = [dot(k, q, rowrow) * (factor * LOG2E) + bias_now for q, k, _, _, bias_now, _ in blocks]
        turned = [block[3].T for block in blocks]
        grad_weights = [dot(block[2], x, rowcol) for x, block in zip(turned, blocks)]
        highest = [jnp.max(x, axis=0, keepdims=True) for x in scores]
        powers = [jnp.exp2(x - y) for x, y in zip(scores, highest)]
        summed = [jnp.sum(x, axis=0, keepdims=True) for x in powers]
        weights = [x * (block[5] / y) for x, y, block in zip(powers, summed, blocks)]
        half_weights = [x.astype(jnp.bfloat16) for x in weights]
        attended = [dot(block[2], x, colcol) for x, block in zip(half_weights, blocks)]
        dv = [dot(x, block[3], rowcol) for x, block in zip(half_weights, blocks)]
        row_dot = [
            jnp.sum(x.astype(jnp.float32) * y.astype(jnp.bfloat16).astype(jnp.float32), axis=0, keepdims=True)
            for x, y in zip(turned, attended)
        ]
        grad_scores = [(x * (y - z)).astype(jnp.bfloat16) for x, y, z in zip(weights, grad_weights, row_dot)]
        dk = [dot(x, block[0], rowcol) for x, block in zip(grad_scores, blocks)]
        dq = [dot(x, block[1], colcol) for x, block in zip(grad_scores, blocks)]
        for n, totals in enumerate((dq, dk)):
            terms = sum(x * block[n].astype(jnp.float32) for x, block in zip(totals, blocks))
            gain_acc[n] += jnp.sum(terms.reshape(rows // 8, 8, DH), axis=0)
        return [tuple(x.astype(jnp.bfloat16) for x in result) for result in zip(dq, dk, dv)]

    batch = 2 * SLOTS if heads % (2 * SLOTS) == 0 else GROUP

    @pl.loop(0, heads // batch)
    def _(b):
        spots = [b * batch + i for i in range(batch)]
        results = attend([(*(whole(ref, head) for ref in operands), bias[2], owned[2]) for head in spots])
        for head, result in zip(spots, results):
            for a in range(3):
                local[a, :, columns(head)] = result[a]

    def crossing(s, g):
        own = mine[s] > 0.5
        found = []
        for i in range(SLOTS):
            head = g * GROUP + jnp.where(right[s], i, GROUP - 1 - i)
            there = [
                within(i * far_tiles[s] + t - far_base[s]) for t in range(tiles)
            ]
            parts = []
            for a, ref in enumerate(operands):
                other = jnp.concatenate([fwd_recv[s][g][a, t] for t in there], axis=0)
                parts.append(jnp.where(own, whole(ref, head), other))
            real = jnp.where(i < own_count[s], 1.0, 0.0)
            found.append((*parts, bias[s], owned[s] * real))
        return found

    def pack_back(s, g):
        for t in range(room):
            slot, at = back_slots[s][t]
            tile = far_base[s] + at
            tile = jnp.where(tile > tiles - 1, tiles - 1, tile)
            for a in range(3):
                ret_send[s, g, a, t] = stage[s, g, a, slot * tiles + tile]

    def cross(*parts):
        for s, g in parts:
            @pl.when(exists[s])
            def _(s=s, g=g):
                forward(s, g).wait_recv()
        return attend([block for s, g in parts for block in crossing(s, g)])

    def keep(results, *parts):
        for n, (s, g) in enumerate(parts):
            for i in range(SLOTS):
                for a in range(3):
                    result = results[n * SLOTS + i][a]
                    stage[s, g, a, i * tiles:(i + 1) * tiles] = result.reshape(tiles, TILE, DH)

    def send_back(s, g):
        pack_back(s, g)

        @pl.when(exists[s])
        def _():
            backward(s, g).start()

    @pl.when(head_of_line)
    def _():
        pl.semaphore_wait(here, n_seq - 1)
        for d in range(1, n_dp):
            pl.semaphore_signal(lines, inc=1, device_id={"dp": lax.rem(my_dp + d, n_dp)})

    last = groups - 1
    inner = [(1, g) for g in range(last)]
    for parts in (inner, [(1, last)], *([(0, g)] for g in range(last))):
        keep(cross(*parts), *parts)
        for part in parts:
            if part != (0, last - 1):
                send_back(*part)
        if parts == inner:
            @pl.when(head_of_line)
            def _():
                pl.semaphore_wait(lines, n_dp - 1)
                for d in range(1, n_seq):
                    pl.semaphore_signal(ready, inc=1, device_id={"seq": d})
    results = cross((0, last))

    count = n_seq * n_dp
    place = my_dp * n_seq + me
    gains = (qgain_ref, kgain_ref)
    for n in range(2):
        all_gain[place, n:n + 1] = jnp.sum(gain_acc[n], axis=0, keepdims=True) * factor / gains[n][...]

    def share(dp, seq):
        return pltpu.make_async_remote_copy(
            all_gain.at[place], all_gain.at[place], gain_ss, gain_rs, device_id={"dp": dp, "seq": seq}
        )

    def share_with(seq):
        for d in range(1, n_dp):
            share(lax.rem(my_dp + d, n_dp), seq).start()

    def share_all():
        others = all_gain.at[pl.ds(0, count - 1)]
        return pltpu.make_async_remote_copy(others, others, gain_ss, gain_rs, device_id={"seq": partner[1]})

    @pl.when(me > 0)
    def _():
        pl.semaphore_wait(ready, 1)

    if count <= 64:
        for n in range(n_seq):
            share_with(n)
            if n > 0:
                share(my_dp, lax.rem(me + n, n_seq)).start()
    else:
        @pl.loop(0, n_seq)
        def _(n):
            share_with(n)

        @pl.loop(1, n_seq)
        def _(n):
            share(my_dp, lax.rem(me + n, n_seq)).start()
    send_back(0, last - 1)
    keep(results, (0, last))
    send_back(0, last)

    def merge(g):
        for s in range(2):
            @pl.when(exists[s])
            def _(s=s):
                backward(s, g).wait_recv()
        own_rows = [mine[s] > 0.5 for s in range(2)]
        for i in range(GROUP):
            head = g * GROUP + i
            cols = columns(head)
            merged = []
            for a in range(3):
                value = local[a, :, cols]
                for s in range(2):
                    slot = jnp.where(right[s], i, GROUP - 1 - i)
                    kept = stage[s, g, a, pl.ds(jnp.minimum(slot, SLOTS - 1) * tiles, tiles)].reshape(rows, DH)
                    there = [
                        within((GROUP - 1 - slot) * my_tiles[s] + t - my_base[s])
                        for t in range(tiles)
                    ]
                    back = jnp.concatenate([ret_recv[s][g][a, t] for t in there], axis=0)
                    ours = jnp.full((rows, DH), slot) < own_count[s]
                    chosen = jnp.where(ours, kept, back)
                    value = jnp.where(own_rows[s], chosen, value)
                merged.append(value)
            for n, (src, gain) in enumerate(((xq, qgain_ref), (xk, kgain_ref))):
                outputs[n][0, :, cols] = norm_back(
                    merged[n].astype(jnp.float32), src[:, cols].astype(jnp.float32), rinv[n, head], gain[...] * factor
                )
            dv_ref[0, :, cols] = merged[2]

    for g in range(groups):
        merge(g)
    share_all().wait_recv()
    gain_ref[...] = jnp.sum(all_gain[...], axis=0)
    share_all().wait_send()

    for s in range(2):
        @pl.when(exists[s])
        def _(s=s):
            for g in range(groups):
                forward(s, g).wait_send()
                backward(s, g).wait_send()


def write_back(dq_in, dk_in, dv_in, gain_in, dq_ref, dk_ref, dv_ref, gain_ref, sem):
    copies = [
        pltpu.make_async_copy(held, out, sem.at[i])
        for i, (held, out) in enumerate(
            ((dq_in, dq_ref), (dk_in, dk_ref), (dv_in, dv_ref), (gain_in, gain_ref))
        )
    ]
    for copy in copies:
        copy.start()
    for copy in copies:
        copy.wait()


def body(query_rows, key_rows, value_rows, out_grad, query_gain, key_gain, lengths):
    rows, width = query_rows.shape[1:]
    samples = lengths.shape[1]
    n_seq, n_dp = lax.axis_size("seq"), lax.axis_size("dp")
    heads = width // DH
    groups = heads // GROUP
    counts, room = division(rows // TILE)
    big = jax.ShapeDtypeStruct((1, rows, width), jnp.bfloat16)
    anywhere = pl.BlockSpec(memory_space=pl.ANY)
    hbm = pl.BlockSpec(memory_space=pltpu.HBM)
    vmem = pl.BlockSpec(memory_space=pltpu.VMEM)
    dma = pltpu.SemaphoreType.DMA
    half = jnp.bfloat16
    limit = 67043328 - 3 * big.size * 2 - 131072
    shapes = (big, big, big, jax.ShapeDtypeStruct((2, DH), jnp.float32))
    results = pl.pallas_call(
        functools.partial(kernel, rows, width, samples, n_seq, n_dp, room, counts),
        out_shape=tuple(pltpu.VMEM(x.shape, x.dtype) for x in shapes),
        in_specs=[hbm] * 4 + [hbm] * 3,
        out_specs=(vmem, vmem, vmem, vmem),
        scratch_shapes=[
            pltpu.VMEM((1, DH), jnp.float32),
            pltpu.VMEM((1, DH), jnp.float32),
            pltpu.SMEM((1, samples), jnp.int32),
            *[pltpu.VMEM((rows, width), half)] * 4,
            *[pltpu.VMEM((heads * rows // TILE, TILE, DH), half)] * 4,
            pltpu.VMEM((2, heads, rows, DH), jnp.float32),
            pltpu.VMEM((3, rows, width), half),
            pltpu.VMEM((3, rows, rows), jnp.float32),
            pltpu.VMEM((3, 1, rows), jnp.float32),
            pltpu.VMEM((2, rows, DH), half),
            pltpu.VMEM((2, groups, 4, room, TILE, DH), half),
            pltpu.VMEM((2, groups, 3, room, TILE, DH), half),
            pltpu.VMEM((2, groups, 3, SLOTS * rows // TILE, TILE, DH), half),
            pltpu.VMEM((2, 8, DH), jnp.float32),
            pltpu.VMEM((n_seq * n_dp, 2, DH), jnp.float32),
            *[pltpu.VMEM((4, room, TILE, DH), half)] * (2 * groups),
            *[pltpu.VMEM((3, room, TILE, DH), half)] * (2 * groups),
            dma((groups + 1, 4)),
            dma((2, groups)),
            dma((2, groups)),
            dma((2, groups)),
            dma((2, groups)),
            dma(()),
            dma(()),
            *[pltpu.SemaphoreType.REGULAR] * 3,
        ],
        compiler_params=pltpu.CompilerParams(collective_id=0, has_side_effects=True, vmem_limit_bytes=limit),
    )(
        query_rows, key_rows, value_rows, out_grad,
        query_gain.reshape(1, DH), key_gain.reshape(1, DH), lengths,
    )
    return pl.pallas_call(
        write_back,
        out_shape=shapes,
        in_specs=[anywhere] * 4,
        out_specs=(anywhere,) * 4,
        scratch_shapes=[dma((4,))],
        compiler_params=pltpu.CompilerParams(vmem_limit_bytes=8 << 20),
    )(*results)


def solution(mesh):
    placed = (
        P("dp", "seq", None),
        P("dp", "seq", None),
        P("dp", "seq", None),
        P("dp", "seq", None),
        P(),
        P(),
        P("dp", None),
    )
    return jax.shard_map(
        body,
        mesh=mesh,
        in_specs=placed,
        out_specs=(P("dp", "seq", None), P("dp", "seq", None), P("dp", "seq", None), P()),
        check_vma=False,
    )
```

```python
import functools

import jax
import jax.numpy as jnp
from jax import lax
from jax.experimental import pallas as pl
from jax.experimental.pallas import tpu as pltpu
from jax.sharding import PartitionSpec as P

DH = 128
EPSILON = 1e-06
MASKED = -1e30
TILE = 16
GROUP = 4
SLOTS = GROUP - 1
LOG2E = 1.4426950408889634


def division(tiles):
    counts, most = [SLOTS], 0
    for left in range(1, tiles + 1):
        right = tiles + 1 - left
        need, taken = min((max(t * left, (GROUP - t) * right), -t) for t in range(1, GROUP))
        counts.append(-taken)
        most = max(most, need)
    return counts, most


def norm_back(grad, rows_in, inverse, gain):
    unit = rows_in * inverse
    scaled = grad * gain
    inner = jnp.mean(scaled * unit, axis=1, keepdims=True)
    return (inverse * (scaled - unit * inner)).astype(jnp.bfloat16)


def kernel(rows, width, samples, n_seq, n_dp, room, counts, *refs):
    heads = width // DH
    groups = heads // GROUP
    tiles = rows // TILE
    factor = DH ** (-0.5)
    refs = list(refs)

    def take(n):
        got = refs[:n]
        del refs[:n]
        return got

    q_in, k_in, v_in, g_in, qgain_in, kgain_in, len_in = take(7)
    dq_ref, dk_ref, dv_ref, gain_ref = take(4)
    qgain_ref, kgain_ref, len_ref = take(3)
    xq, xk, xv, xg, qn, kn, vt, gt, rinv, local, bias, owned, mine = take(13)
    fwd_send, ret_send, stage, gain_acc, all_gain = take(5)
    fwd_recv = [take(groups) for _ in range(2)]
    ret_recv = [take(groups) for _ in range(2)]
    (load_sem, fwd_ss, fwd_rs, ret_ss, ret_rs, gain_ss, gain_rs, here, lines, ready) = take(10)

    me = lax.axis_index("seq")
    my_dp = lax.axis_index("dp")
    odd = lax.rem(me, 2)
    outputs = (dq_ref, dk_ref, dv_ref)

    right = (odd == 0, odd == 1)
    partner = (jnp.where(odd == 0, me - 1, me + 1), jnp.where(odd == 0, me + 1, me - 1))
    exists = tuple((p >= 0) & (p < n_seq) for p in partner)

    def columns(head):
        return pl.ds(pl.multiple_of(head * DH, DH), DH)

    def span(g):
        return pl.ds(g * GROUP * DH, GROUP * DH)

    small = [
        pltpu.make_async_copy(src, dst, load_sem.at[groups, i])
        for i, (src, dst) in enumerate(((len_in, len_ref), (qgain_in, qgain_ref), (kgain_in, kgain_ref)))
    ]
    loads = [
        [
            pltpu.make_async_copy(src.at[0, :, span(g)], dst.at[:, span(g)], load_sem.at[g, i])
            for i, (src, dst) in enumerate(((q_in, xq), (k_in, xk), (v_in, xv), (g_in, xg)))
        ]
        for g in range(groups)
    ]

    barrier = pltpu.get_barrier_semaphore()
    for s in range(2):
        @pl.when(exists[s])
        def _(s=s):
            pl.semaphore_signal(barrier, inc=1, device_id={"seq": partner[s]})
    small[0].start()
    for load in loads[0]:
        load.start()
    head_of_line = me == 0

    @pl.when(head_of_line)
    def _():
        for d in range(1, n_dp):
            pl.semaphore_signal(barrier, inc=1, device_id={"dp": lax.rem(my_dp + d, n_dp)})
        for d in range(2, n_seq):
            pl.semaphore_signal(barrier, inc=1, device_id={"seq": d})

    expected = jnp.where(head_of_line, n_dp - 1, jnp.where(me >= 2, 1, 0))
    expected = expected + jnp.where(exists[0], 1, 0) + jnp.where(exists[1], 1, 0)
    for load in small[1:]:
        load.start()
    for g in range(1, groups):
        for load in loads[g]:
            load.start()
    for load in (*small, *loads[0]):
        load.wait()

    far = rows * n_seq + 2 * rows
    first = me * rows

    edge = [jnp.where(right[s], first, first + rows) for s in range(2)]
    start = [jnp.int32(0), jnp.int32(0)]
    end = [jnp.int32(far), jnp.int32(far)]
    total = jnp.int32(0)
    for i in range(samples):
        total = total + len_ref[0, i]
        for s in range(2):
            end[s] = jnp.where(total > edge[s], jnp.minimum(end[s], total), end[s])
            start[s] = jnp.where(total <= edge[s], total, start[s])

    def tile_count(n):
        return sum(jnp.where(n > t * TILE, 1, 0) for t in range(tiles))

    my_rows, far_rows, my_tiles, far_tiles, my_base, far_base, own_count = [], [], [], [], [], [], []
    for s in range(2):
        before = edge[s] - start[s]
        after = jnp.where(before > 0, end[s] - edge[s], 0)
        mr = jnp.where(right[s], after, before)
        fr = jnp.where(right[s], before, after)
        mt = tile_count(mr)
        ft = tile_count(fr)
        lt = jnp.where(right[s], ft, mt)
        taken = jnp.int32(counts[0])
        for n in range(1, len(counts)):
            if counts[n] != counts[n - 1]:
                taken = jnp.where(lt >= n, counts[n], taken)
        my_rows.append(mr)
        far_rows.append(fr)
        my_tiles.append(mt)
        far_tiles.append(ft)
        my_base.append(jnp.where(right[s], 0, tiles - mt))
        far_base.append(jnp.where(right[s], tiles - ft, 0))
        own_count.append(jnp.where(right[s], taken, GROUP - taken))

    def inside(s, at):
        low = jnp.where(right[s], 0, rows - my_rows[s])
        high = jnp.where(right[s], my_rows[s], rows)
        return (at >= low) & (at < high)

    def outside(s, at):
        low = jnp.where(right[s], rows - far_rows[s], 0)
        high = jnp.where(right[s], rows, far_rows[s])
        return (at >= low) & (at < high)

    def within(t):
        return jnp.where(t < 0, 0, jnp.where(t > room - 1, room - 1, t))

    def split(t, per):
        slot = jnp.int32(0)
        for n in range(1, SLOTS):
            slot = slot + jnp.where(t >= n * per, 1, 0)
        return slot, t - slot * per

    operands = (qn, kn, vt, gt)

    def whole(ref, head):
        return ref[pl.ds(head * tiles, tiles)].reshape(rows, DH)

    out_slots = [[split(t, my_tiles[s]) for t in range(room)] for s in range(2)]
    back_slots = [[split(t, far_tiles[s]) for t in range(room)] for s in range(2)]

    def pack(s, g):
        for t in range(room):
            slot, at = out_slots[s][t]
            tile = my_base[s] + at
            tile = jnp.where(tile > tiles - 1, tiles - 1, tile)
            head = g * GROUP + jnp.where(right[s], GROUP - 1 - slot, slot)
            for a, ref in enumerate(operands):
                fwd_send[s, g, a, t] = ref[head * tiles + tile]

    def forward(s, g):
        return pltpu.make_async_remote_copy(
            fwd_send.at[s, g], fwd_recv[s][g], fwd_ss.at[s, g], fwd_rs.at[s, g], device_id={"seq": partner[s]}
        )

    def backward(s, g):
        return pltpu.make_async_remote_copy(
            ret_send.at[s, g], ret_recv[s][g], ret_ss.at[s, g], ret_rs.at[s, g], device_id={"seq": partner[s]}
        )

    for g in range(groups):
        if g > 0:
            for load in loads[g]:
                load.wait()
        for i in range(GROUP):
            head = g * GROUP + i
            for n, (src, dst, gain) in enumerate(((xq, qn, qgain_ref), (xk, kn, kgain_ref))):
                x = src[:, columns(head)].astype(jnp.float32)
                r = lax.rsqrt(jnp.mean(x * x, axis=1, keepdims=True) + EPSILON)
                normed = (x * r * gain[...]).astype(jnp.bfloat16)
                dst[pl.ds(head * tiles, tiles)] = normed.reshape(tiles, TILE, DH)
                rinv[n, head] = jnp.broadcast_to(r, (rows, DH))
            for src, dst in ((xv, vt), (xg, gt)):
                dst[pl.ds(head * tiles, tiles)] = src[:, columns(head)].reshape(tiles, TILE, DH)
        pack(0, g)
        if g == 0:
            pl.semaphore_wait(barrier, expected)
        for s in range(2):
            if s == 1:
                pack(1, g)

            @pl.when(exists[s])
            def _(s=s, g=g):
                forward(s, g).start()
            if (g, s) == (0, 0):
                @pl.when(me > 0)
                def _():
                    pl.semaphore_signal(here, inc=1, device_id={"seq": 0})
    col = lax.broadcasted_iota(jnp.int32, (rows, 1), 0)
    row = lax.broadcasted_iota(jnp.int32, (1, rows), 1)
    start_col = jnp.zeros((rows, 1), jnp.int32)
    start_row = jnp.zeros((1, rows), jnp.int32)
    total = jnp.int32(0)
    for i in range(samples):
        total = total + len_ref[0, i]
        start_col = jnp.where(total <= col + first, total, start_col)
        start_row = jnp.where(total <= row + first, total, start_row)
    bias[2] = jnp.where(start_col == start_row, 0.0, MASKED)
    owned[2] = jnp.where(inside(0, row) | inside(1, row), 0.0, 1.0)
    square = lax.broadcasted_iota(jnp.int32, (rows, DH), 0)
    for s in range(2):
        valid_col = inside(s, col) | outside(s, col)
        valid_row = inside(s, row) | outside(s, row)
        bias[s] = jnp.where(valid_col, 0.0, MASKED) + jnp.where(valid_row, 0.0, MASKED)
        owned[s] = jnp.where(valid_row, 1.0, 0.0)
        mine[s] = jnp.where(inside(s, square), 1.0, 0.0).astype(jnp.bfloat16)
    gain_acc[...] = jnp.zeros_like(gain_acc)

    for s in range(2):
        @pl.when(jnp.logical_not(exists[s]))
        def _(s=s):
            for g in range(groups):
                fwd_recv[s][g][...] = jnp.zeros_like(fwd_recv[s][g])
                ret_recv[s][g][...] = jnp.zeros_like(ret_recv[s][g])

    rowrow = (((1,), (1,)), ((), ()))
    rowcol = (((1,), (0,)), ((), ()))
    colcol = (((0,), (0,)), ((), ()))
    dot = functools.partial(lax.dot_general, preferred_element_type=jnp.float32)

    def attend(blocks):
        scores = [dot(k, q, rowrow) * (factor * LOG2E) + bias_now for q, k, _, _, bias_now, _ in blocks]
        turned = [block[3].T for block in blocks]
        grad_weights = [dot(block[2], x, rowcol) for x, block in zip(turned, blocks)]
        highest = [jnp.max(x, axis=0, keepdims=True) for x in scores]
        powers = [jnp.exp2(x - y) for x, y in zip(scores, highest)]
        summed = [jnp.sum(x, axis=0, keepdims=True) for x in powers]
        weights = [x * (block[5] / y) for x, y, block in zip(powers, summed, blocks)]
        half_weights = [x.astype(jnp.bfloat16) for x in weights]
        attended = [dot(block[2], x, colcol) for x, block in zip(half_weights, blocks)]
        dv = [dot(x, block[3], rowcol) for x, block in zip(half_weights, blocks)]
        row_dot = [
            jnp.sum(x.astype(jnp.float32) * y.astype(jnp.bfloat16).astype(jnp.float32), axis=0, keepdims=True)
            for x, y in zip(turned, attended)
        ]
        grad_scores = [(x * (y - z)).astype(jnp.bfloat16) for x, y, z in zip(weights, grad_weights, row_dot)]
        dk = [dot(x, block[0], rowcol) for x, block in zip(grad_scores, blocks)]
        dq = [dot(x, block[1], colcol) for x, block in zip(grad_scores, blocks)]
        for n, totals in enumerate((dq, dk)):
            terms = sum(x * block[n].astype(jnp.float32) for x, block in zip(totals, blocks))
            gain_acc[n] += jnp.sum(terms.reshape(rows // 8, 8, DH), axis=0)
        return [tuple(x.astype(jnp.bfloat16) for x in result) for result in zip(dq, dk, dv)]

    batch = 2 * SLOTS if heads % (2 * SLOTS) == 0 else GROUP

    @pl.loop(0, heads // batch)
    def _(b):
        spots = [b * batch + i for i in range(batch)]
        results = attend([(*(whole(ref, head) for ref in operands), bias[2], owned[2]) for head in spots])
        for head, result in zip(spots, results):
            for a in range(3):
                local[a, :, columns(head)] = result[a]

    def crossing(s, g):
        own = mine[s] > 0.5
        found = []
        for i in range(SLOTS):
            head = g * GROUP + jnp.where(right[s], i, GROUP - 1 - i)
            there = [
                within(i * far_tiles[s] + t - far_base[s]) for t in range(tiles)
            ]
            parts = []
            for a, ref in enumerate(operands):
                other = jnp.concatenate([fwd_recv[s][g][a, t] for t in there], axis=0)
                parts.append(jnp.where(own, whole(ref, head), other))
            real = jnp.where(i < own_count[s], 1.0, 0.0)
            found.append((*parts, bias[s], owned[s] * real))
        return found

    def pack_back(s, g):
        for t in range(room):
            slot, at = back_slots[s][t]
            tile = far_base[s] + at
            tile = jnp.where(tile > tiles - 1, tiles - 1, tile)
            for a in range(3):
                ret_send[s, g, a, t] = stage[s, g, a, slot * tiles + tile]

    def cross(*parts):
        for s, g in parts:
            @pl.when(exists[s])
            def _(s=s, g=g):
                forward(s, g).wait_recv()
        results = attend([block for s, g in parts for block in crossing(s, g)])
        for n, (s, g) in enumerate(parts):
            for i in range(SLOTS):
                for a in range(3):
                    result = results[n * SLOTS + i][a]
                    stage[s, g, a, i * tiles:(i + 1) * tiles] = result.reshape(tiles, TILE, DH)

    def send_back(s, g):
        pack_back(s, g)

        @pl.when(exists[s])
        def _():
            backward(s, g).start()

    @pl.when(head_of_line)
    def _():
        pl.semaphore_wait(here, n_seq - 1)
        for d in range(1, n_dp):
            pl.semaphore_signal(lines, inc=1, device_id={"dp": lax.rem(my_dp + d, n_dp)})

    last = groups - 1
    inner = [(1, g) for g in range(last)]
    for parts in (inner, [(1, last)], *([(0, g)] for g in range(last))):
        cross(*parts)
        for part in parts:
            if part != (0, last - 1):
                send_back(*part)
        if parts == inner:
            @pl.when(head_of_line)
            def _():
                pl.semaphore_wait(lines, n_dp - 1)
                for d in range(1, n_seq):
                    pl.semaphore_signal(ready, inc=1, device_id={"seq": d})
    cross((0, last))

    count = n_seq * n_dp
    place = my_dp * n_seq + me
    gains = (qgain_ref, kgain_ref)
    for n in range(2):
        all_gain[place, n:n + 1] = jnp.sum(gain_acc[n], axis=0, keepdims=True) * factor / gains[n][...]

    def share(dp, seq):
        return pltpu.make_async_remote_copy(
            all_gain.at[place], all_gain.at[place], gain_ss, gain_rs, device_id={"dp": dp, "seq": seq}
        )

    def share_with(seq):
        for d in range(1, n_dp):
            share(lax.rem(my_dp + d, n_dp), seq).start()

    def share_all():
        others = all_gain.at[pl.ds(0, count - 1)]
        return pltpu.make_async_remote_copy(others, others, gain_ss, gain_rs, device_id={"seq": partner[1]})

    @pl.when(me > 0)
    def _():
        pl.semaphore_wait(ready, 1)

    if count <= 64:
        for n in range(n_seq):
            if n < n_seq - 1:
                share(my_dp, jnp.where(n >= me, n + 1, n)).start()
            share_with(n)
    else:
        @pl.loop(0, n_seq)
        def _(n):
            share_with(n)

        @pl.loop(1, n_seq)
        def _(n):
            share(my_dp, lax.rem(me + n, n_seq)).start()
    send_back(0, last - 1)
    send_back(0, last)

    def merge(g):
        for s in range(2):
            @pl.when(exists[s])
            def _(s=s):
                backward(s, g).wait_recv()
        own_rows = [mine[s] > 0.5 for s in range(2)]
        for i in range(GROUP):
            head = g * GROUP + i
            cols = columns(head)
            merged = []
            for a in range(3):
                value = local[a, :, cols]
                for s in range(2):
                    slot = jnp.where(right[s], i, GROUP - 1 - i)
                    kept = stage[s, g, a, pl.ds(jnp.minimum(slot, SLOTS - 1) * tiles, tiles)].reshape(rows, DH)
                    there = [
                        within((GROUP - 1 - slot) * my_tiles[s] + t - my_base[s])
                        for t in range(tiles)
                    ]
                    back = jnp.concatenate([ret_recv[s][g][a, t] for t in there], axis=0)
                    ours = jnp.full((rows, DH), slot) < own_count[s]
                    chosen = jnp.where(ours, kept, back)
                    value = jnp.where(own_rows[s], chosen, value)
                merged.append(value)
            for n, (src, gain) in enumerate(((xq, qgain_ref), (xk, kgain_ref))):
                outputs[n][0, :, cols] = norm_back(
                    merged[n].astype(jnp.float32), src[:, cols].astype(jnp.float32), rinv[n, head], gain[...] * factor
                )
            dv_ref[0, :, cols] = merged[2]

    for g in range(groups):
        merge(g)
    share_all().wait_recv()
    gain_ref[...] = jnp.sum(all_gain[...], axis=0)
    share_all().wait_send()

    for s in range(2):
        @pl.when(exists[s])
        def _(s=s):
            for g in range(groups):
                forward(s, g).wait_send()
                backward(s, g).wait_send()


def write_back(dq_in, dk_in, dv_in, gain_in, dq_ref, dk_ref, dv_ref, gain_ref, sem):
    copies = [
        pltpu.make_async_copy(held, out, sem.at[i])
        for i, (held, out) in enumerate(
            ((dq_in, dq_ref), (dk_in, dk_ref), (dv_in, dv_ref), (gain_in, gain_ref))
        )
    ]
    for copy in copies:
        copy.start()
    for copy in copies:
        copy.wait()


def body(query_rows, key_rows, value_rows, out_grad, query_gain, key_gain, lengths):
    rows, width = query_rows.shape[1:]
    samples = lengths.shape[1]
    n_seq, n_dp = lax.axis_size("seq"), lax.axis_size("dp")
    heads = width // DH
    groups = heads // GROUP
    counts, room = division(rows // TILE)
    big = jax.ShapeDtypeStruct((1, rows, width), jnp.bfloat16)
    anywhere = pl.BlockSpec(memory_space=pl.ANY)
    hbm = pl.BlockSpec(memory_space=pltpu.HBM)
    vmem = pl.BlockSpec(memory_space=pltpu.VMEM)
    dma = pltpu.SemaphoreType.DMA
    half = jnp.bfloat16
    limit = 67043328 - 3 * big.size * 2 - 131072
    shapes = (big, big, big, jax.ShapeDtypeStruct((2, DH), jnp.float32))
    results = pl.pallas_call(
        functools.partial(kernel, rows, width, samples, n_seq, n_dp, room, counts),
        out_shape=tuple(pltpu.VMEM(x.shape, x.dtype) for x in shapes),
        in_specs=[hbm] * 4 + [hbm] * 3,
        out_specs=(vmem, vmem, vmem, vmem),
        scratch_shapes=[
            pltpu.VMEM((1, DH), jnp.float32),
            pltpu.VMEM((1, DH), jnp.float32),
            pltpu.SMEM((1, samples), jnp.int32),
            *[pltpu.VMEM((rows, width), half)] * 4,
            *[pltpu.VMEM((heads * rows // TILE, TILE, DH), half)] * 4,
            pltpu.VMEM((2, heads, rows, DH), jnp.float32),
            pltpu.VMEM((3, rows, width), half),
            pltpu.VMEM((3, rows, rows), jnp.float32),
            pltpu.VMEM((3, 1, rows), jnp.float32),
            pltpu.VMEM((2, rows, DH), half),
            pltpu.VMEM((2, groups, 4, room, TILE, DH), half),
            pltpu.VMEM((2, groups, 3, room, TILE, DH), half),
            pltpu.VMEM((2, groups, 3, SLOTS * rows // TILE, TILE, DH), half),
            pltpu.VMEM((2, 8, DH), jnp.float32),
            pltpu.VMEM((n_seq * n_dp, 2, DH), jnp.float32),
            *[pltpu.VMEM((4, room, TILE, DH), half)] * (2 * groups),
            *[pltpu.VMEM((3, room, TILE, DH), half)] * (2 * groups),
            dma((groups + 1, 4)),
            dma((2, groups)),
            dma((2, groups)),
            dma((2, groups)),
            dma((2, groups)),
            dma(()),
            dma(()),
            *[pltpu.SemaphoreType.REGULAR] * 3,
        ],
        compiler_params=pltpu.CompilerParams(collective_id=0, has_side_effects=True, vmem_limit_bytes=limit),
    )(
        query_rows, key_rows, value_rows, out_grad,
        query_gain.reshape(1, DH), key_gain.reshape(1, DH), lengths,
    )
    return pl.pallas_call(
        write_back,
        out_shape=shapes,
        in_specs=[anywhere] * 4,
        out_specs=(anywhere,) * 4,
        scratch_shapes=[dma((4,))],
        compiler_params=pltpu.CompilerParams(vmem_limit_bytes=8 << 20),
    )(*results)


def solution(mesh):
    placed = (
        P("dp", "seq", None),
        P("dp", "seq", None),
        P("dp", "seq", None),
        P("dp", "seq", None),
        P(),
        P(),
        P("dp", None),
    )
    return jax.shard_map(
        body,
        mesh=mesh,
        in_specs=placed,
        out_specs=(P("dp", "seq", None), P("dp", "seq", None), P("dp", "seq", None), P()),
        check_vma=False,
    )
```
